512 devices in a mesh: fsdp: 64 (over z, y_hi, core), ctx: 8 (over x, y_lo).
Axes of the slice: x: 4, y: 4 (y_hi: 2, y_lo: 2; y = y_hi * 2 + y_lo), z: 16, core: 2. Of those that a mesh axis runs over, the one named last changes fastest.
Arguments:
- queries: bfloat16 [64, 1024, 1536], P('fsdp', 'ctx'), may hold values from -1.6953125 to 1.6953125
- key_states: bfloat16 [64, 1024, 1536], P('fsdp', 'ctx'), may hold values from -1.6953125 to 1.6953125
- value_states: bfloat16 [64, 1024, 1536], P('fsdp', 'ctx'), may hold values from -6 to 6
- attn_out: bfloat16 [64, 1024, 1536], P('fsdp', 'ctx'), may hold values from -6 to 6
- log_norm: bfloat16 [64, 1024, 12], P('fsdp', 'ctx'), may hold values from 3 to 4.5
- out_grad: bfloat16 [64, 1024, 3072], P('fsdp', 'ctx'), may hold values from -6 to 6
- proj_weight: bfloat16 [1536, 3072], P('fsdp', 'ctx'), may hold values from -0.109375 to 0.109375
- tile_mask: int32 [64, 12, 16, 16], P('fsdp'), may hold values from 0 to 1, as said below
Outputs:
- grad_query: bfloat16 [64, 1024, 1536], P('fsdp', 'ctx')
- grad_key: bfloat16 [64, 1024, 1536], P('fsdp', 'ctx')
- grad_value: bfloat16 [64, 1024, 1536], P('fsdp', 'ctx')
The draws below stay inside these ranges and needn't reach their ends.
Inputs may be any that keep to these rules, and one draw needn't show every extreme that they name: tile_mask[c, h, i, j] = 1 lets the query tokens of tile i attend to the key tokens of tile j in head h; a tile is 64 consecutive tokens; every tile attends to itself.
All inputs are finite; a program needn't handle non-finite values.
Results may differ from the reference program's by a relative error of at most 0.014.
Values may be sent and summed in bfloat16 or wider, within the bound.
No kernel may reach another device: no remote copies, remote signals or barrier semaphores. Data moves between devices by JAX's collectives and lax.ppermute only.
A program may use at most 64 MiB of HBM per device.

```python
import jax
import jax.numpy as jnp
from jax import lax

D = 3072
H = 12
HD = 128
TILE = 64
TOK_DEV = 128
CLIPS = 64
SEQ = 1024
HID = 1536
NT = 16
N_CTX = 8


def draw_tile_mask(key, part):
    rate_key, roll_key = jax.random.split(key, 2)
    rates = jax.random.randint(rate_key, (CLIPS, 1, NT, 1), 30, 900)
    rolls = jax.random.randint(roll_key, (CLIPS, H, NT, NT), 0, 1000)
    diagonal_term = jnp.arange(NT)[:, None] == jnp.arange(NT)[None, :]
    return jnp.where((rolls < rates) | diagonal_term[None, None], 1, 0).astype(jnp.int32)


def steps_of(key, shape, cuts, least, largest):
    level = 1.0
    for dim, shards_of in cuts:
        draws = jax.random.uniform(jax.random.fold_in(jax.random.fold_in(key, 6), dim), (shards_of,), jnp.float32, least / len(cuts), largest / len(cuts))
        level = level * jnp.repeat(jnp.exp(draws), shape[dim] // shards_of).reshape((-1,) + (1,) * (len(shape) - 1 - dim))
    return level


def normal_values(key, extent, deviation, most, cuts=(), held_as=jnp.bfloat16):
    gain = steps_of(key, extent, cuts, -0.22, 0.18) if cuts else 1.0
    values = jax.random.normal(key, extent, jnp.float32) * deviation * gain
    return jnp.minimum(jnp.maximum(values, -most), most).astype(held_as)


def setup_inputs(seed: int = 0) -> dict:
    arg_keys = jax.random.split(jax.random.key(seed), 9)
    queries = jnp.clip(jax.random.uniform(arg_keys[0], (CLIPS, SEQ, HID), jnp.float32, -1.6953125, 1.6953125) * steps_of(arg_keys[0], (CLIPS, SEQ, HID), ((0, 64), (1, 8)), -0.4, 0.0), -1.6953125, 1.6953125).astype(jnp.bfloat16)
    key_states = jnp.clip(jax.random.uniform(arg_keys[1], (CLIPS, SEQ, HID), jnp.float32, -1.6953125, 1.6953125) * steps_of(arg_keys[1], (CLIPS, SEQ, HID), ((0, 64), (1, 8)), -0.4, 0.0), -1.6953125, 1.6953125).astype(jnp.bfloat16)
    value_states = normal_values(arg_keys[2], (CLIPS, SEQ, HID), 1.0, 6.0, ((0, 64), (1, 8)))
    attn_out = normal_values(arg_keys[3], (CLIPS, SEQ, HID), 1.0, 6.0, ((0, 64), (1, 8)))
    log_norm = jnp.clip(3.0 + 1.5 * jax.random.uniform(arg_keys[4], (CLIPS, SEQ, H), jnp.float32) ** steps_of(arg_keys[4], (CLIPS, SEQ, H), ((0, 64), (1, 8)), -0.2, 0.2), 3.0, 4.5).astype(jnp.bfloat16)
    out_grad = normal_values(arg_keys[5], (CLIPS, SEQ, D), 1.0, 6.0, ((0, 64), (1, 8)))
    proj_weight = normal_values(arg_keys[6], (HID, D), D ** -0.5, 0.109375, ((0, 64), (1, 8)))
    tile_mask = draw_tile_mask(jax.random.fold_in(arg_keys[8], 71), 0)
    return {"queries": queries, "key_states": key_states, "value_states": value_states, "attn_out": attn_out, "log_norm": log_norm, "out_grad": out_grad, "proj_weight": proj_weight, "tile_mask": tile_mask}


def round_trip(array):
    return lax.optimization_barrier(array.astype(jnp.bfloat16)).astype(jnp.float32)


def reference(queries, key_states, value_states, attn_out, log_norm, out_grad, proj_weight, tile_mask):
    score_scale = HD ** -0.5
    slab_width = D // N_CTX
    weight_blocks = proj_weight.astype(jnp.float32).reshape(H * HD, N_CTX, slab_width)
    tile_ids = jnp.arange(SEQ, dtype=jnp.int32) // TILE

    def one_clip(inputs):
        query_row_block, key_rows, value_rows, out_rows, norm_rows, grad_rows, table = inputs
        grad_blocks = grad_rows.astype(jnp.float32).reshape(SEQ, N_CTX, slab_width)
        weight_part = jnp.einsum('lbw,hbw->blh', grad_blocks, weight_blocks)
        attn_grad = jnp.sum(round_trip(weight_part), axis=0).astype(jnp.bfloat16)
        gradient_by_head = attn_grad.astype(jnp.float32).reshape(SEQ, H, HD)
        out_heads = out_rows.astype(jnp.float32).reshape(SEQ, H, HD)
        row_dots = round_trip(jnp.sum(gradient_by_head * out_heads, axis=-1))
        allowed = table[:, tile_ids[:, None], tile_ids[None, :]].astype(jnp.float32)
        query_head_rows = query_row_block.astype(jnp.float32).reshape(SEQ, H, HD)
        key_head_rows = key_rows.astype(jnp.float32).reshape(SEQ, H, HD)
        value_head_rows = value_rows.astype(jnp.float32).reshape(SEQ, H, HD)
        scores = jnp.einsum('thd,shd->hts', query_head_rows, key_head_rows) * score_scale
        attn_prob = jnp.exp(scores - norm_rows.astype(jnp.float32).T[:, :, None]) * allowed
        prob_grad = jnp.einsum('thd,shd->hts', gradient_by_head, value_head_rows)
        score_grad = attn_prob * (prob_grad - row_dots.T[:, :, None])
        probability_per_round = round_trip(attn_prob)
        gradient_per_round = round_trip(score_grad)
        by_query = probability_per_round.reshape(H, N_CTX, TOK_DEV, SEQ)
        grad_by_query = gradient_per_round.reshape(H, N_CTX, TOK_DEV, SEQ)
        value_part = jnp.einsum('hbts,bthd->bshd', by_query, gradient_by_head.reshape(N_CTX, TOK_DEV, H, HD))
        key_part = score_scale * jnp.einsum('hbts,bthd->bshd', grad_by_query, query_head_rows.reshape(N_CTX, TOK_DEV, H, HD))
        query_part = score_scale * jnp.einsum('htbs,bshd->bthd', gradient_per_round.reshape(H, SEQ, N_CTX, TOK_DEV), key_head_rows.reshape(N_CTX, TOK_DEV, H, HD))
        grad_value = jnp.sum(round_trip(value_part), axis=0).astype(jnp.bfloat16).reshape(SEQ, H * HD)
        grad_key = jnp.sum(round_trip(key_part), axis=0).astype(jnp.bfloat16).reshape(SEQ, H * HD)
        grad_query = jnp.sum(round_trip(query_part), axis=0).astype(jnp.bfloat16).reshape(SEQ, H * HD)
        return grad_query, grad_key, grad_value

    grad_query, grad_key, grad_value = lax.map(one_clip, (queries, key_states, value_states, attn_out, log_norm, out_grad, tile_mask))
    return (grad_query, grad_key, grad_value)
```

```python
import functools
import math

import jax
import jax.numpy as jnp
from jax import lax
from jax.experimental import pallas as pl
from jax.experimental.pallas import tpu as pltpu
from jax.sharding import Mesh, PartitionSpec as P

BF = jnp.bfloat16
F32 = jnp.float32
HD = 128
TILE = 64
SCALE = HD**-0.5
LOG2E = math.log2(math.e)

QA, KA, VA, OA, KC, VC, QC, OC, NR = 0, 128, 256, 384, 512, 640, 768, 832, 896
IN_ROWS = 912
MID = 192
GQA, GKA, GVA, GKC, GVC, GQC = 0, 128, 256, 384, 512, 640
OUT_ROWS = 704

NT_DIMS = (((1,), (1,)), ((), ()))
NN_DIMS = (((1,), (0,)), ((), ()))
TN_DIMS = (((0,), (0,)), ((), ()))


def dot(a, b, dims):
    return lax.dot_general(a, b, dims, preferred_element_type=F32)


def pack_kernel(q_ref, k_ref, v_ref, o_ref, n_ref, g_ref, in_ref, slab_ref):
    slab_ref[0] = g_ref[...]
    for j in range(2):
        own = slice(HD * j, HD * (j + 1))
        shared = slice(2 * HD, 3 * HD)
        half = slice(TILE * j, TILE * (j + 1))
        in_ref[j, QA : QA + 128] = q_ref[:, own]
        in_ref[j, KA : KA + 128] = k_ref[:, own]
        in_ref[j, VA : VA + 128] = v_ref[:, own]
        in_ref[j, OA : OA + 128] = o_ref[:, own]
        in_ref[j, KC : KC + 128] = k_ref[:, shared]
        in_ref[j, VC : VC + 128] = v_ref[:, shared]
        in_ref[j, QC : QC + 64] = q_ref[half, shared]
        in_ref[j, OC : OC + 64] = o_ref[half, shared]
        in_ref[j, NR:IN_ROWS] = n_ref[0, j]


def pack(q, k, v, o, norm_rows, out_grad):
    wide = pl.BlockSpec((128, 3 * HD), lambda i: (0, i))
    return pl.pallas_call(
        pack_kernel,
        grid=(4,),
        in_specs=[wide] * 4
        + [pl.BlockSpec((1, 2, 16, 128), lambda i: (i, 0, 0, 0)), pl.BlockSpec((128, 768), lambda i: (0, i))],
        out_specs=(
            pl.BlockSpec((2, IN_ROWS, 128), lambda i: (i, 0, 0)),
            pl.BlockSpec((1, 128, 768), lambda i: (i, 0, 0)),
        ),
        out_shape=(
            jax.ShapeDtypeStruct((8, IN_ROWS, 128), BF),
            jax.ShapeDtypeStruct((4, 128, 768), BF),
        ),
        name="pack",
    )(q, k, v, o, norm_rows, out_grad)


def project_kernel(core_ref, own_ref, other_ref, g_ref, out_ref, w_ref):
    mine = core_ref[0] == 0
    for z in range(4):
        for yh in range(2):
            for yl in range(2):
                a = own_ref[yh, yl, z]
                b = other_ref[yh, yl, z]
                for c in range(2):
                    row = 24 * (4 * z + 2 * yh + c)
                    piece = jnp.where(mine, a, b) if c == 0 else jnp.where(mine, b, a)
                    w_ref[row : row + 24, 384 * yl : 384 * (yl + 1)] = piece
    g = g_ref[...].reshape(512, 768)
    part = dot(g, w_ref[...], NT_DIMS).astype(BF)
    for x in range(4):
        rows = slice(128 * x, 128 * (x + 1))
        for j in range(2):
            base = MID * x
            out_ref[j, base : base + 128] = part[rows, HD * j : HD * (j + 1)]
            out_ref[j, base + 128 : base + MID] = part[128 * x + 64 * j : 128 * x + 64 * (j + 1), 2 * HD :]


def project(core, own, other, slab):
    shard = pl.BlockSpec((2, 2, 4, 24, 384), lambda i: (0, 0, i, 0, 0))
    return pl.pallas_call(
        project_kernel,
        grid=(4,),
        in_specs=[
            pl.BlockSpec(memory_space=pltpu.SMEM),
            shard,
            shard,
            pl.BlockSpec((4, 128, 768), lambda i: (0, 0, 0)),
        ],
        out_specs=pl.BlockSpec((2, 4 * MID, 128), lambda i: (i, 0, 0)),
        out_shape=jax.ShapeDtypeStruct((8, 4 * MID, 128), BF),
        scratch_shapes=[pltpu.VMEM((384, 768), BF)],
        name="project",
    )(core, own, other, slab)


def attend_unit(in_ref, mid_ref, mask_ref, out_ref, dk_ref, dv_ref, per, rows, norm_row, outs):
    q0, o0, k0, v0, m0 = rows
    gq0, gk0, gv0 = outs
    group = 256 // per
    keys = 1024
    chunk = 256
    for b in range(8 // group):
        sources = range(group * b, group * (b + 1))
        q = jnp.concatenate([in_ref[s, q0 : q0 + per] for s in sources], axis=0)
        o = jnp.concatenate([in_ref[s, o0 : o0 + per] for s in sources], axis=0)
        pieces = []
        for s in sources:
            base = MID * (s // 2) + m0
            total = mid_ref[s % 2, base : base + per].astype(F32)
            for x in range(1, 4):
                total = total + mid_ref[2 * x + s % 2, base : base + per].astype(F32)
            pieces.append(total.astype(BF))
        g = jnp.concatenate(pieces, axis=0)
        product = g.astype(F32) * o.astype(F32)
        dots = lax.dot_general(
            jnp.ones((8, 128), F32), product, NT_DIMS, precision=lax.Precision.HIGHEST, preferred_element_type=F32
        )[0:1]
        dots = dots.astype(BF).astype(F32)
        norm = norm_row(b)
        dq = jnp.zeros((HD, 256), F32)
        for n in range(keys // chunk):
            src = slice(2 * n, 2 * n + 2)
            k = in_ref[src, k0 : k0 + 128].reshape(chunk, HD)
            v = in_ref[src, v0 : v0 + 128].reshape(chunk, HD)
            scores = dot(k, q, NT_DIMS)
            prob = jnp.exp2(scores * (SCALE * LOG2E) - norm)
            allowed = mask_ref[4 * n : 4 * (n + 1), 256 * b : 256 * (b + 1)]
            prob = (prob.reshape(4, TILE, 256) * allowed[:, None, :]).reshape(chunk, 256)
            score_grad = prob * (dot(v, g, NT_DIMS) - dots)
            prob = prob.astype(BF)
            score_grad = score_grad.astype(BF)
            dv = dot(prob, g, NN_DIMS)
            dk = dot(score_grad, q, NN_DIMS)
            at = slice(chunk * n, chunk * (n + 1))
            if b == 0:
                dv_ref[at] = dv
                dk_ref[at] = dk
            else:
                dv_ref[at] += dv
                dk_ref[at] += dk
            dq = dq + dot(k, score_grad, TN_DIMS)
        dq = (dq.T * SCALE).astype(BF)
        for e, s in enumerate(sources):
            out_ref[s, gq0 : gq0 + per] = dq[per * e : per * (e + 1)]
    for s in range(8):
        at = slice(128 * s, 128 * (s + 1))
        out_ref[s, gk0 : gk0 + 128] = (dk_ref[at] * SCALE).astype(BF)
        out_ref[s, gv0 : gv0 + 128] = dv_ref[at].astype(BF)


def attend_kernel(y_ref, in_ref, mid_ref, mask_a_ref, mask_c_ref, out_ref, dk_ref, dv_ref):
    second = y_ref[0] == 1

    def norm_a(b):
        parts = [in_ref[s, NR : NR + 16].astype(F32)[0:1] for s in (2 * b, 2 * b + 1)]
        return jnp.concatenate(parts, axis=1) * LOG2E

    def norm_c(b):
        parts = []
        for s in range(4 * b, 4 * b + 4):
            row = in_ref[s, NR : NR + 16].astype(F32)[1:2]
            parts.append(jnp.where(second, row[:, 64:], row[:, :64]))
        return jnp.concatenate(parts, axis=1) * LOG2E

    attend_unit(
        in_ref, mid_ref, mask_a_ref, out_ref, dk_ref, dv_ref, 128, (QA, OA, KA, VA, 0), norm_a, (GQA, GKA, GVA)
    )
    attend_unit(
        in_ref, mid_ref, mask_c_ref, out_ref, dk_ref, dv_ref, 64, (QC, OC, KC, VC, 128), norm_c, (GQC, GKC, GVC)
    )


def attend(y_index, arrived, partial, mask_a, mask_c):
    whole = pl.BlockSpec(memory_space=pltpu.VMEM)
    return pl.pallas_call(
        attend_kernel,
        in_specs=[pl.BlockSpec(memory_space=pltpu.SMEM), whole, whole, whole, whole],
        out_specs=whole,
        out_shape=jax.ShapeDtypeStruct((8, OUT_ROWS, 128), BF),
        scratch_shapes=[pltpu.VMEM((1024, 128), F32), pltpu.VMEM((1024, 128), F32)],
        name="attend",
    )(y_index, arrived, partial, mask_a, mask_c)


def merge_kernel(in_ref, gq_ref, gk_ref, gv_ref):
    for j in range(2):
        own = slice(HD * j, HD * (j + 1))
        gq_ref[0, :, own] = in_ref[j, GQA : GQA + 128]
        gk_ref[0, :, own] = in_ref[j, GKA : GKA + 128]
        gv_ref[0, :, own] = in_ref[j, GVA : GVA + 128]
        gq_ref[0, TILE * j : TILE * (j + 1), 2 * HD :] = in_ref[j, GQC : GQC + 64]
    for ref, at in ((gk_ref, GKC), (gv_ref, GVC)):
        total = in_ref[0, at : at + 128].astype(F32) + in_ref[1, at : at + 128].astype(F32)
        ref[0, :, 2 * HD :] = total.astype(BF)


def merge(arrived):
    out = pl.BlockSpec((1, 128, 3 * HD), lambda i: (0, 0, i))
    shape = jax.ShapeDtypeStruct((1, 128, 1536), BF)
    return pl.pallas_call(
        merge_kernel,
        grid=(4,),
        in_specs=[pl.BlockSpec((2, OUT_ROWS, 128), lambda i: (i, 0, 0))],
        out_specs=(out, out, out),
        out_shape=(shape, shape, shape),
        name="merge",
    )(arrived)


def exchange(array, axes):
    return lax.all_to_all(array, axes, split_axis=0, concat_axis=0, tiled=True)


def spread(array, axes, count):
    return exchange(jnp.broadcast_to(array[None], (count,) + array.shape), axes)


def gather_weight(proj_weight):
    own = spread(proj_weight, "z", 16)
    own = spread(own, ("yh", "yl"), 4).reshape(2, 2, 16, 24, 384)
    other = lax.ppermute(own, "core", [(0, 1), (1, 0)])
    return own, other


def mask_rows(tile_mask):
    x, y = lax.axis_index("x"), lax.axis_index("yl")
    table = tile_mask[0].astype(F32).transpose(0, 2, 1)
    whole = lax.dynamic_index_in_dim(table, 3 * x + y, 0, keepdims=False)
    shared = lax.dynamic_index_in_dim(table, 3 * x + 2, 0, keepdims=False).reshape(16, 8, 2)
    shared = lax.dynamic_index_in_dim(shared, y, 2, keepdims=False)
    return jnp.repeat(whole, TILE, axis=1), jnp.repeat(shared, TILE, axis=1)


def norm_table(log_norm):
    rows = log_norm[0].T.reshape(4, 3, 128)
    both = jnp.stack([rows[:, :2], jnp.broadcast_to(rows[:, 2:], (4, 2, 128))], axis=2)
    return jnp.pad(both, ((0, 0), (0, 0), (0, 14), (0, 0)))


def after_weight(q, k, v, o, log_norm, out_grad, own, other, core, tile_mask):
    sent, slab = pack(q[0], k[0], v[0], o[0], norm_table(log_norm), out_grad[0])
    slab = exchange(slab, "x")
    arrived = exchange(sent, ("x", "yl"))
    partial = exchange(project(core, own, other, slab), ("x", "yl"))
    mask_a, mask_c = mask_rows(tile_mask)
    y_index = lax.axis_index("yl").reshape(1)
    result = exchange(attend(y_index, arrived, partial, mask_a, mask_c), ("x", "yl"))
    return merge(result)


def local(queries, key_states, value_states, attn_out, log_norm, out_grad, proj_weight, tile_mask):
    own, other = gather_weight(proj_weight)
    core = lax.axis_index("core").reshape(1)
    return after_weight(
        queries, key_states, value_states, attn_out, log_norm, out_grad, own, other, core, tile_mask
    )


def solution(mesh):
    inner = Mesh(mesh.devices.reshape(16, 2, 2, 4, 2), ("z", "yh", "core", "x", "yl"))
    clips, tokens = ("z", "yh", "core"), ("x", "yl")
    rows = P(clips, tokens, None)
    return jax.shard_map(
        local,
        mesh=inner,
        in_specs=(rows,) * 6 + (P(clips, tokens), P(clips, None, None, None)),
        out_specs=(rows, rows, rows),
        check_vma=False,
    )
```

```python
import math

import jax
import jax.numpy as jnp
from jax import lax
from jax.experimental import pallas as pl
from jax.experimental.pallas import tpu as pltpu
from jax.sharding import Mesh, PartitionSpec as P


BF = jnp.bfloat16
F32 = jnp.float32
HD = 128
TILE = 64
SCALE = HD**-0.5
LOG2E = math.log2(math.e)

QA, KA, VA, OA, KC, VC, QC, OC, NR = 0, 128, 256, 384, 512, 640, 768, 832, 896
IN_ROWS = 912
SLAB = 768
GRANT = 16 << 20
MID = 192
GQA, GKA, GVA, GKC, GVC, GQC = 0, 128, 256, 384, 512, 640
OUT_ROWS = 704

NT_DIMS = (((1,), (1,)), ((), ()))
NN_DIMS = (((1,), (0,)), ((), ()))
TN_DIMS = (((0,), (0,)), ((), ()))


def dot(a, b, dims):
    return lax.dot_general(a, b, dims, preferred_element_type=F32)


def pack_kernel(me_ref, q_ref, k_ref, v_ref, o_ref, n_ref, g_ref, *out_refs):
    for d, out_ref in enumerate(out_refs):
        to = jnp.bitwise_xor(me_ref[0], d)
        x, y = to // 2, to % 2
        base = 0 if d % 2 else SLAB
        own = pl.ds(pl.multiple_of(HD * (3 * x + y), HD), HD)
        shared = pl.ds(pl.multiple_of(HD * (3 * x + 2), HD), HD)
        half = pl.ds(pl.multiple_of(TILE * y, TILE), TILE)
        if base:
            for e in range(6):
                columns = pl.ds(pl.multiple_of(768 * x + 128 * e, 128), 128)
                out_ref[128 * e : 128 * (e + 1)] = g_ref[:, columns]
        for ref, at in ((q_ref, QA), (k_ref, KA), (v_ref, VA), (o_ref, OA)):
            out_ref[base + at : base + at + 128] = ref[:, own]
        for ref, at in ((k_ref, KC), (v_ref, VC)):
            out_ref[base + at : base + at + 128] = ref[:, shared]
        for ref, at in ((q_ref, QC), (o_ref, OC)):
            out_ref[base + at : base + at + 64] = ref[half, shared]
        line = lax.broadcasted_iota(jnp.int32, (16, 12), 0)
        head = lax.broadcasted_iota(jnp.int32, (16, 12), 1)
        wanted = jnp.where(line == 0, 3 * x + y, 3 * x + 2)
        pick = jnp.where((head == wanted) & (line < 2), 1.0, 0.0).astype(BF)
        out_ref[base + NR : base + IN_ROWS] = dot(pick, n_ref[...], NN_DIMS).astype(BF)


def pack(me, q, k, v, o, norms, out_grad):
    whole = pl.BlockSpec(memory_space=pltpu.VMEM)
    return pl.pallas_call(
        pack_kernel,
        in_specs=[pl.BlockSpec(memory_space=pltpu.SMEM)] + [whole] * 6,
        out_specs=(whole,) * 8,
        out_shape=tuple(jax.ShapeDtypeStruct((IN_ROWS + (0 if d % 2 else SLAB), 128), BF) for d in range(8)),
        compiler_params=pltpu.CompilerParams(vmem_limit_bytes=GRANT),
        name="pack",
    )(me, q, k, v, o, norms, out_grad)


def project_kernel(where_ref, own_ref, other_ref, g0_ref, g1_ref, g2_ref, g3_ref, out_ref, w_ref, g_ref):
    @pl.when(pl.program_id(0) == 0)
    def _():
        for e, ref in enumerate((g0_ref, g1_ref, g2_ref, g3_ref)):
            source = jnp.bitwise_xor(where_ref[1], e)
            for n in range(6):
                g_ref[source, :, 128 * n : 128 * (n + 1)] = ref[128 * n : 128 * (n + 1)]

    mine = where_ref[0] == 0
    for z in range(4):
        for yh in range(2):
            for yl in range(2):
                a = own_ref[yh, yl, z]
                b = other_ref[yh, yl, z]
                for c in range(2):
                    row = 24 * (4 * z + 2 * yh + c)
                    piece = jnp.where(mine, a, b) if c == 0 else jnp.where(mine, b, a)
                    w_ref[row : row + 24, 384 * yl : 384 * (yl + 1)] = piece
    g = g_ref[...].reshape(512, 768)
    part = dot(g, w_ref[...], NT_DIMS).astype(BF)
    for x in range(4):
        rows = slice(128 * x, 128 * (x + 1))
        for j in range(2):
            base = MID * x
            out_ref[j, base : base + 128] = part[rows, HD * j : HD * (j + 1)]
            out_ref[j, base + 128 : base + MID] = part[128 * x + 64 * j : 128 * x + 64 * (j + 1), 2 * HD :]


def project(where, own, other, slabs):
    shard = pl.BlockSpec((2, 2, 4, 24, 384), lambda i: (0, 0, i, 0, 0))
    slab = pl.BlockSpec((SLAB, 128), lambda i: (0, 0))
    return pl.pallas_call(
        project_kernel,
        grid=(4,),
        in_specs=[pl.BlockSpec(memory_space=pltpu.SMEM), shard, shard] + [slab] * 4,
        out_specs=pl.BlockSpec((2, 4 * MID, 128), lambda i: (i, 0, 0)),
        out_shape=jax.ShapeDtypeStruct((8, 4 * MID, 128), BF),
        scratch_shapes=[pltpu.VMEM((384, 768), BF), pltpu.VMEM((4, 128, 768), BF)],
        compiler_params=pltpu.CompilerParams(vmem_limit_bytes=GRANT),
        name="project",
    )(where, own, other, *slabs)


def attend_unit(in_ref, mid_ref, mask_ref, out_ref, dk_ref, dv_ref, per, rows, norm_row, outs):
    q0, o0, k0, v0, m0 = rows
    gq0, gk0, gv0 = outs
    group = 256 // per
    keys = 1024
    chunk = 256
    for b in range(8 // group):
        sources = range(group * b, group * (b + 1))
        q = jnp.concatenate([in_ref[s, q0 : q0 + per] for s in sources], axis=0)
        o = jnp.concatenate([in_ref[s, o0 : o0 + per] for s in sources], axis=0)
        pieces = []
        for s in sources:
            base = MID * (s // 2) + m0
            total = mid_ref[s % 2, base : base + per].astype(F32)
            for x in range(1, 4):
                total = total + mid_ref[2 * x + s % 2, base : base + per].astype(F32)
            pieces.append(total.astype(BF))
        g = jnp.concatenate(pieces, axis=0)
        product = g.astype(F32) * o.astype(F32)
        dots = lax.dot_general(
            jnp.ones((8, 128), F32), product, NT_DIMS, precision=lax.Precision.HIGHEST, preferred_element_type=F32
        )[0:1]
        dots = dots.astype(BF).astype(F32)
        norm = norm_row(b)
        dq = jnp.zeros((HD, 256), F32)
        for n in range(keys // chunk):
            src = slice(2 * n, 2 * n + 2)
            k = in_ref[src, k0 : k0 + 128].reshape(chunk, HD)
            v = in_ref[src, v0 : v0 + 128].reshape(chunk, HD)
            scores = dot(k, q, NT_DIMS)
            prob = jnp.exp2(scores * (SCALE * LOG2E) - norm)
            allowed = mask_ref[4 * n : 4 * (n + 1), 256 * b : 256 * (b + 1)]
            prob = (prob.reshape(4, TILE, 256) * allowed[:, None, :]).reshape(chunk, 256)
            score_grad = prob * (dot(v, g, NT_DIMS) - dots)
            prob = prob.astype(BF)
            score_grad = score_grad.astype(BF)
            dv = dot(prob, g, NN_DIMS)
            dk = dot(score_grad, q, NN_DIMS)
            at = slice(chunk * n, chunk * (n + 1))
            if b == 0:
                dv_ref[at] = dv
                dk_ref[at] = dk
            else:
                dv_ref[at] += dv
                dk_ref[at] += dk
            dq = dq + dot(k, score_grad, TN_DIMS)
        dq = (dq.T * SCALE).astype(BF)
        for e, s in enumerate(sources):
            out_ref[s, gq0 : gq0 + per] = dq[per * e : per * (e + 1)]
    for s in range(8):
        at = slice(128 * s, 128 * (s + 1))
        out_ref[s, gk0 : gk0 + 128] = (dk_ref[at] * SCALE).astype(BF)
        out_ref[s, gv0 : gv0 + 128] = dv_ref[at].astype(BF)


def attend_kernel(me_ref, *refs):
    sent_refs = refs[:8]
    mid_ref, mask_a_ref, mask_c_ref, out_ref, in_ref, dk_ref, dv_ref, sems = refs[8:]
    copies = []
    for d, ref in enumerate(sent_refs):
        source = ref if d % 2 else ref.at[pl.ds(SLAB, IN_ROWS)]
        copies.append(pltpu.make_async_copy(source, in_ref.at[jnp.bitwise_xor(me_ref[0], d)], sems.at[d]))
        copies[-1].start()
    for copy in copies:
        copy.wait()
    second = me_ref[0] % 2 == 1

    def norm_a(b):
        parts = [in_ref[s, NR : NR + 16].astype(F32)[0:1] for s in (2 * b, 2 * b + 1)]
        return jnp.concatenate(parts, axis=1) * LOG2E

    def norm_c(b):
        parts = []
        for s in range(4 * b, 4 * b + 4):
            row = in_ref[s, NR : NR + 16].astype(F32)[1:2]
            parts.append(jnp.where(second, row[:, 64:], row[:, :64]))
        return jnp.concatenate(parts, axis=1) * LOG2E

    attend_unit(
        in_ref, mid_ref, mask_a_ref, out_ref, dk_ref, dv_ref, 128, (QA, OA, KA, VA, 0), norm_a, (GQA, GKA, GVA)
    )
    attend_unit(
        in_ref, mid_ref, mask_c_ref, out_ref, dk_ref, dv_ref, 64, (QC, OC, KC, VC, 128), norm_c, (GQC, GKC, GVC)
    )


def attend(me, arrived, partial, mask_a, mask_c):
    whole = pl.BlockSpec(memory_space=pltpu.VMEM)
    return pl.pallas_call(
        attend_kernel,
        in_specs=[pl.BlockSpec(memory_space=pltpu.SMEM)]
        + [pl.BlockSpec(memory_space=pl.ANY)] * 8
        + [whole, whole, whole],
        out_specs=whole,
        out_shape=jax.ShapeDtypeStruct((8, OUT_ROWS, 128), BF),
        scratch_shapes=[
            pltpu.VMEM((8, IN_ROWS, 128), BF),
            pltpu.VMEM((1024, 128), F32),
            pltpu.VMEM((1024, 128), F32),
            pltpu.SemaphoreType.DMA((8,)),
        ],
        compiler_params=pltpu.CompilerParams(vmem_limit_bytes=GRANT),
        name="attend",
    )(me, *arrived, partial, mask_a, mask_c)


def merge_kernel(in_ref, gq_ref, gk_ref, gv_ref):
    for j in range(2):
        own = slice(HD * j, HD * (j + 1))
        gq_ref[0, :, own] = in_ref[j, GQA : GQA + 128]
        gk_ref[0, :, own] = in_ref[j, GKA : GKA + 128]
        gv_ref[0, :, own] = in_ref[j, GVA : GVA + 128]
        gq_ref[0, TILE * j : TILE * (j + 1), 2 * HD :] = in_ref[j, GQC : GQC + 64]
    for ref, at in ((gk_ref, GKC), (gv_ref, GVC)):
        total = in_ref[0, at : at + 128].astype(F32) + in_ref[1, at : at + 128].astype(F32)
        ref[0, :, 2 * HD :] = total.astype(BF)


def merge(arrived):
    out = pl.BlockSpec((1, 128, 3 * HD), lambda i: (0, 0, i))
    shape = jax.ShapeDtypeStruct((1, 128, 1536), BF)
    return pl.pallas_call(
        merge_kernel,
        grid=(4,),
        in_specs=[pl.BlockSpec((2, OUT_ROWS, 128), lambda i: (i, 0, 0))],
        out_specs=(out, out, out),
        out_shape=(shape, shape, shape),
        compiler_params=pltpu.CompilerParams(vmem_limit_bytes=GRANT),
        name="merge",
    )(arrived)


def exchange(array, axes):
    return lax.all_to_all(array, axes, split_axis=0, concat_axis=0, tiled=True)


def spread(array, axes, count):
    return exchange(jnp.broadcast_to(array[None], (count,) + array.shape), axes)


def gather_weight(proj_weight):
    own = spread(proj_weight, "z", 16)
    own = spread(own, ("yh", "yl"), 4).reshape(2, 2, 16, 24, 384)
    other = lax.ppermute(own, "core", [(0, 1), (1, 0)])
    return own, other


def mask_kernel(where_ref, table_ref, whole_ref, shared_ref):
    x, y = where_ref[0] // 2, where_ref[0] % 2
    for ref, head in ((whole_ref, 3 * x + y), (shared_ref, 3 * x + 2)):
        tile = lax.broadcasted_iota(jnp.int32, (16, ref.shape[1]), 0)
        group = lax.broadcasted_iota(jnp.int32, (16, ref.shape[1]), 1) // TILE
        of_lane = group if ref is whole_ref else 2 * group + y
        spread_out = jnp.where(tile == of_lane, 1.0, 0.0)
        ref[...] = dot(table_ref[0, head].astype(F32), spread_out, TN_DIMS)


def mask_rows(me, tile_mask):
    whole = pl.BlockSpec(memory_space=pltpu.VMEM)
    return pl.pallas_call(
        mask_kernel,
        in_specs=[pl.BlockSpec(memory_space=pltpu.SMEM), whole],
        out_specs=(whole, whole),
        out_shape=(jax.ShapeDtypeStruct((16, 1024), F32), jax.ShapeDtypeStruct((16, 512), F32)),
        compiler_params=pltpu.CompilerParams(vmem_limit_bytes=GRANT),
        name="mask",
    )(me, tile_mask)


def swap(array, d):
    return lax.ppermute(array, ("x", "yl"), [(s, s ^ d) for s in range(8)])


def after_weight(q, k, v, o, log_norm, out_grad, own, other, core, tile_mask):
    x, y = lax.axis_index("x"), lax.axis_index("yl")
    me = (2 * x + y).reshape(1)
    where = jnp.stack([core, x])
    sent = pack(me, q[0], k[0], v[0], o[0], log_norm[0].T, out_grad[0])
    arrived = [sent[d] if d == 0 else swap(sent[d], d) for d in range(8)]
    partial = exchange(project(where, own, other, arrived[::2]), ("x", "yl"))
    mask_a, mask_c = mask_rows(me, tile_mask)
    result = exchange(attend(me, arrived, partial, mask_a, mask_c), ("x", "yl"))
    return merge(result)


def local(queries, key_states, value_states, attn_out, log_norm, out_grad, proj_weight, tile_mask):
    own, other = gather_weight(proj_weight)
    return after_weight(
        queries,
        key_states,
        value_states,
        attn_out,
        log_norm,
        out_grad,
        own,
        other,
        lax.axis_index("core"),
        tile_mask,
    )


def solution(mesh):
    inner = Mesh(mesh.devices.reshape(16, 2, 2, 4, 2), ("z", "yh", "core", "x", "yl"))
    clips, tokens = ("z", "yh", "core"), ("x", "yl")
    rows = P(clips, tokens, None)
    return jax.shard_map(
        local,
        mesh=inner,
        in_specs=(rows,) * 6 + (P(clips, tokens), P(clips, None, None, None)),
        out_specs=(rows, rows, rows),
        check_vma=False,
    )
```

```python
import functools
import math

import jax
import jax.numpy as jnp
from jax import lax
from jax.experimental import pallas as pl
from jax.experimental.pallas import tpu as pltpu
from jax.sharding import Mesh, PartitionSpec as P


BF = jnp.bfloat16
F32 = jnp.float32
HD = 128
TILE = 64
SCALE = HD**-0.5
LOG2E = math.log2(math.e)

QA, KA, VA, OA, KC, VC, QC, OC, NR = 0, 128, 256, 384, 512, 640, 768, 832, 896
IN_ROWS = 912
SLAB = 768
GRANT = 16 << 20
WHOLE_GRANT = 62 << 20
MID = 192
GQA, GKA, GVA, GKC, GVC, GQC = 0, 128, 256, 384, 512, 640
OUT_ROWS = 704

NT_DIMS = (((1,), (1,)), ((), ()))
NN_DIMS = (((1,), (0,)), ((), ()))
TN_DIMS = (((0,), (0,)), ((), ()))


def dot(a, b, dims):
    return lax.dot_general(a, b, dims, preferred_element_type=F32)


def load(sources, targets, sems):
    copies = [pltpu.make_async_copy(a, b, sems.at[n]) for n, (a, b) in enumerate(zip(sources, targets, strict=True))]
    for copy in copies:
        copy.start()
    for copy in copies:
        copy.wait()


def pack_kernel(me_ref, q_hbm, k_hbm, v_hbm, o_hbm, n_hbm, g_hbm, *refs):
    out_refs = refs[:8]
    q_ref, k_ref, v_ref, o_ref, n_ref, g_ref, sems = refs[8:]
    load((q_hbm, k_hbm, v_hbm, o_hbm, n_hbm, g_hbm), (q_ref, k_ref, v_ref, o_ref, n_ref, g_ref), sems)
    for d, out_ref in enumerate(out_refs):
        to = jnp.bitwise_xor(me_ref[0], d)
        x, y = to // 2, to % 2
        base = 0 if d % 2 else SLAB
        own = pl.ds(pl.multiple_of(HD * (3 * x + y), HD), HD)
        shared = pl.ds(pl.multiple_of(HD * (3 * x + 2), HD), HD)
        half = pl.ds(pl.multiple_of(TILE * y, TILE), TILE)
        if base:
            for e in range(6):
                columns = pl.ds(pl.multiple_of(768 * x + 128 * e, 128), 128)
                out_ref[128 * e : 128 * (e + 1)] = g_ref[:, columns]
        for ref, at in ((q_ref, QA), (k_ref, KA), (v_ref, VA), (o_ref, OA)):
            out_ref[base + at : base + at + 128] = ref[:, own]
        for ref, at in ((k_ref, KC), (v_ref, VC)):
            out_ref[base + at : base + at + 128] = ref[:, shared]
        for ref, at in ((q_ref, QC), (o_ref, OC)):
            out_ref[base + at : base + at + 64] = ref[half, shared]
        line = lax.broadcasted_iota(jnp.int32, (16, 12), 0)
        head = lax.broadcasted_iota(jnp.int32, (16, 12), 1)
        wanted = jnp.where(line == 0, 3 * x + y, 3 * x + 2)
        pick = jnp.where((head == wanted) & (line < 2), 1.0, 0.0).astype(BF)
        out_ref[base + NR : base + IN_ROWS] = dot(pick, n_ref[...], NN_DIMS).astype(BF)


def pack(me, q, k, v, o, norms, out_grad):
    whole = pl.BlockSpec(memory_space=pltpu.VMEM)
    return pl.pallas_call(
        pack_kernel,
        in_specs=[pl.BlockSpec(memory_space=pltpu.SMEM)] + [pl.BlockSpec(memory_space=pl.ANY)] * 6,
        out_specs=(whole,) * 8,
        out_shape=tuple(jax.ShapeDtypeStruct((IN_ROWS + (0 if d % 2 else SLAB), 128), BF) for d in range(8)),
        scratch_shapes=[
            *[pltpu.VMEM((128, 1536), BF)] * 4,
            pltpu.VMEM((12, 128), BF),
            pltpu.VMEM((128, 3072), BF),
            pltpu.SemaphoreType.DMA((6,)),
        ],
        compiler_params=pltpu.CompilerParams(vmem_limit_bytes=WHOLE_GRANT),
        name="pack",
    )(me, q, k, v, o, norms, out_grad)


def project_kernel(where_ref, own_ref, other_ref, g0_ref, g1_ref, g2_ref, g3_ref, out_ref, w_ref, g_ref):
    @pl.when(pl.program_id(0) == 0)
    def _():
        for e, ref in enumerate((g0_ref, g1_ref, g2_ref, g3_ref)):
            source = jnp.bitwise_xor(where_ref[1], e)
            for n in range(6):
                g_ref[source, :, 128 * n : 128 * (n + 1)] = ref[128 * n : 128 * (n + 1)]

    mine = where_ref[0] == 0
    for z in range(4):
        for yh in range(2):
            for yl in range(2):
                a = own_ref[yh, yl, z]
                b = other_ref[yh, yl, z]
                for c in range(2):
                    row = 24 * (4 * z + 2 * yh + c)
                    piece = jnp.where(mine, a, b) if c == 0 else jnp.where(mine, b, a)
                    w_ref[row : row + 24, 384 * yl : 384 * (yl + 1)] = piece
    g = g_ref[...].reshape(512, 768)
    part = dot(g, w_ref[...], NT_DIMS).astype(BF)
    for x in range(4):
        rows = slice(128 * x, 128 * (x + 1))
        for j in range(2):
            base = MID * x
            out_ref[j, base : base + 128] = part[rows, HD * j : HD * (j + 1)]
            out_ref[j, base + 128 : base + MID] = part[128 * x + 64 * j : 128 * x + 64 * (j + 1), 2 * HD :]


def project(where, own, other, slabs):
    shard = pl.BlockSpec((2, 2, 4, 24, 384), lambda i: (0, 0, i, 0, 0))
    slab = pl.BlockSpec((SLAB, 128), lambda i: (0, 0))
    return pl.pallas_call(
        project_kernel,
        grid=(4,),
        in_specs=[pl.BlockSpec(memory_space=pltpu.SMEM), shard, shard] + [slab] * 4,
        out_specs=pl.BlockSpec((2, 4 * MID, 128), lambda i: (i, 0, 0)),
        out_shape=jax.ShapeDtypeStruct((8, 4 * MID, 128), BF),
        scratch_shapes=[pltpu.VMEM((384, 768), BF), pltpu.VMEM((4, 128, 768), BF)],
        compiler_params=pltpu.CompilerParams(vmem_limit_bytes=GRANT),
        name="project",
    )(where, own, other, *slabs)


def attend_unit(in_ref, mid_ref, mask_ref, out_ref, dk_ref, dv_ref, per, rows, norm_row, outs):
    q0, o0, k0, v0, m0 = rows
    gq0, gk0, gv0 = outs
    group = 256 // per
    keys = 1024
    chunk = 256
    for b in range(8 // group):
        sources = range(group * b, group * (b + 1))
        q = jnp.concatenate([in_ref[s, q0 : q0 + per] for s in sources], axis=0)
        o = jnp.concatenate([in_ref[s, o0 : o0 + per] for s in sources], axis=0)
        pieces = []
        for s in sources:
            base = MID * (s // 2) + m0
            total = mid_ref[s % 2, base : base + per].astype(F32)
            for x in range(1, 4):
                total = total + mid_ref[2 * x + s % 2, base : base + per].astype(F32)
            pieces.append(total.astype(BF))
        g = jnp.concatenate(pieces, axis=0)
        product = g.astype(F32) * o.astype(F32)
        dots = lax.dot_general(
            jnp.ones((8, 128), F32), product, NT_DIMS, precision=lax.Precision.HIGHEST, preferred_element_type=F32
        )[0:1]
        dots = dots.astype(BF).astype(F32)
        norm = norm_row(b)
        dq = jnp.zeros((HD, 256), F32)
        for n in range(keys // chunk):
            src = slice(2 * n, 2 * n + 2)
            k = in_ref[src, k0 : k0 + 128].reshape(chunk, HD)
            v = in_ref[src, v0 : v0 + 128].reshape(chunk, HD)
            scores = dot(k, q, NT_DIMS)
            prob = jnp.exp2(scores * (SCALE * LOG2E) - norm)
            allowed = mask_ref[4 * n : 4 * (n + 1), 256 * b : 256 * (b + 1)]
            prob = (prob.reshape(4, TILE, 256) * allowed[:, None, :]).reshape(chunk, 256)
            score_grad = prob * (dot(v, g, NT_DIMS) - dots)
            prob = prob.astype(BF)
            score_grad = score_grad.astype(BF)
            dv = dot(prob, g, NN_DIMS)
            dk = dot(score_grad, q, NN_DIMS)
            at = slice(chunk * n, chunk * (n + 1))
            if b == 0:
                dv_ref[at] = dv
                dk_ref[at] = dk
            else:
                dv_ref[at] += dv
                dk_ref[at] += dk
            dq = dq + dot(k, score_grad, TN_DIMS)
        dq = (dq.T * SCALE).astype(BF)
        for e, s in enumerate(sources):
            out_ref[s, gq0 : gq0 + per] = dq[per * e : per * (e + 1)]
    for s in range(8):
        at = slice(128 * s, 128 * (s + 1))
        out_ref[s, gk0 : gk0 + 128] = (dk_ref[at] * SCALE).astype(BF)
        out_ref[s, gv0 : gv0 + 128] = dv_ref[at].astype(BF)


def attend_kernel(me_ref, *refs):
    sent_refs = refs[:8]
    mid_ref, mask_a_hbm, mask_c_hbm, out_ref, in_ref, dk_ref, dv_ref, mask_a_ref, mask_c_ref, sems = refs[8:]
    sources = [ref if d % 2 else ref.at[pl.ds(SLAB, IN_ROWS)] for d, ref in enumerate(sent_refs)]
    targets = [in_ref.at[jnp.bitwise_xor(me_ref[0], d)] for d in range(8)]
    load((*sources, mask_a_hbm, mask_c_hbm), (*targets, mask_a_ref, mask_c_ref), sems)
    second = me_ref[0] % 2 == 1

    def norm_a(b):
        parts = [in_ref[s, NR : NR + 16].astype(F32)[0:1] for s in (2 * b, 2 * b + 1)]
        return jnp.concatenate(parts, axis=1) * LOG2E

    def norm_c(b):
        parts = []
        for s in range(4 * b, 4 * b + 4):
            row = in_ref[s, NR : NR + 16].astype(F32)[1:2]
            parts.append(jnp.where(second, row[:, 64:], row[:, :64]))
        return jnp.concatenate(parts, axis=1) * LOG2E

    attend_unit(
        in_ref, mid_ref, mask_a_ref, out_ref, dk_ref, dv_ref, 128, (QA, OA, KA, VA, 0), norm_a, (GQA, GKA, GVA)
    )
    attend_unit(
        in_ref, mid_ref, mask_c_ref, out_ref, dk_ref, dv_ref, 64, (QC, OC, KC, VC, 128), norm_c, (GQC, GKC, GVC)
    )


def attend(me, arrived, partial, mask_a, mask_c):
    whole = pl.BlockSpec(memory_space=pltpu.VMEM)
    return pl.pallas_call(
        attend_kernel,
        in_specs=[pl.BlockSpec(memory_space=pltpu.SMEM)]
        + [pl.BlockSpec(memory_space=pl.ANY)] * 8
        + [whole]
        + [pl.BlockSpec(memory_space=pl.ANY)] * 2,
        out_specs=whole,
        out_shape=jax.ShapeDtypeStruct((8, OUT_ROWS, 128), BF),
        scratch_shapes=[
            pltpu.VMEM((8, IN_ROWS, 128), BF),
            pltpu.VMEM((1024, 128), F32),
            pltpu.VMEM((1024, 128), F32),
            pltpu.VMEM((16, 1024), F32),
            pltpu.VMEM((16, 512), F32),
            pltpu.SemaphoreType.DMA((10,)),
        ],
        compiler_params=pltpu.CompilerParams(vmem_limit_bytes=GRANT),
        name="attend",
    )(me, *arrived, partial, mask_a, mask_c)


def merge_kernel(in_ref, gq_ref, gk_ref, gv_ref):
    for j in range(2):
        own = slice(HD * j, HD * (j + 1))
        gq_ref[0, :, own] = in_ref[j, GQA : GQA + 128]
        gk_ref[0, :, own] = in_ref[j, GKA : GKA + 128]
        gv_ref[0, :, own] = in_ref[j, GVA : GVA + 128]
        gq_ref[0, TILE * j : TILE * (j + 1), 2 * HD :] = in_ref[j, GQC : GQC + 64]
    for ref, at in ((gk_ref, GKC), (gv_ref, GVC)):
        total = in_ref[0, at : at + 128].astype(F32) + in_ref[1, at : at + 128].astype(F32)
        ref[0, :, 2 * HD :] = total.astype(BF)


def merge(arrived):
    out = pl.BlockSpec((1, 128, 3 * HD), lambda i: (0, 0, i))
    shape = jax.ShapeDtypeStruct((1, 128, 1536), BF)
    return pl.pallas_call(
        merge_kernel,
        grid=(4,),
        in_specs=[pl.BlockSpec((2, OUT_ROWS, 128), lambda i: (i, 0, 0))],
        out_specs=(out, out, out),
        out_shape=(shape, shape, shape),
        compiler_params=pltpu.CompilerParams(vmem_limit_bytes=GRANT),
        name="merge",
    )(arrived)


def exchange(array, axes):
    return lax.all_to_all(array, axes, split_axis=0, concat_axis=0, tiled=True)


def spread(array, axes, count):
    return exchange(jnp.broadcast_to(array[None], (count,) + array.shape), axes)


def gather_weight(proj_weight):
    own = spread(proj_weight, "z", 16)
    own = spread(own, ("yh", "yl"), 4).reshape(2, 2, 16, 24, 384)
    other = lax.ppermute(own, "core", [(0, 1), (1, 0)])
    return own, other


def mask_kernel(shared, where_ref, table_ref, out_ref):
    x, y = where_ref[0] // 2, where_ref[0] % 2
    tile = lax.broadcasted_iota(jnp.int32, out_ref.shape, 0)
    group = lax.broadcasted_iota(jnp.int32, out_ref.shape, 1) // TILE
    of_lane = 2 * group + y if shared else group
    head = 3 * x + 2 if shared else 3 * x + y
    out_ref[...] = dot(table_ref[0, head].astype(F32), jnp.where(tile == of_lane, 1.0, 0.0), TN_DIMS)


def mask_rows(me, tile_mask, shared):
    whole = pl.BlockSpec(memory_space=pltpu.VMEM)
    return pl.pallas_call(
        functools.partial(mask_kernel, shared),
        in_specs=[pl.BlockSpec(memory_space=pltpu.SMEM), whole],
        out_specs=whole,
        out_shape=jax.ShapeDtypeStruct((16, 512 if shared else 1024), F32),
        compiler_params=pltpu.CompilerParams(vmem_limit_bytes=GRANT),
        name="mask",
    )(me, tile_mask)


def swap(array, d):
    return lax.ppermute(array, ("x", "yl"), [(s, s ^ d) for s in range(8)])


def after_weight(q, k, v, o, log_norm, out_grad, own, other, core, tile_mask):
    x, y = lax.axis_index("x"), lax.axis_index("yl")
    me = (2 * x + y).reshape(1)
    where = jnp.stack([core, x])
    sent = pack(me, q[0], k[0], v[0], o[0], log_norm[0].T, out_grad[0])
    arrived = [sent[d] if d == 0 else swap(sent[d], d) for d in range(8)]
    partial = exchange(project(where, own, other, arrived[::2]), ("x", "yl"))
    mask_a, mask_c = mask_rows(me, tile_mask, False), mask_rows(me, tile_mask, True)
    result = exchange(attend(me, arrived, partial, mask_a, mask_c), ("x", "yl"))
    return merge(result)


def local(queries, key_states, value_states, attn_out, log_norm, out_grad, proj_weight, tile_mask):
    own, other = gather_weight(proj_weight)
    return after_weight(
        queries,
        key_states,
        value_states,
        attn_out,
        log_norm,
        out_grad,
        own,
        other,
        lax.axis_index("core"),
        tile_mask,
    )


def solution(mesh):
    inner = Mesh(mesh.devices.reshape(16, 2, 2, 4, 2), ("z", "yh", "core", "x", "yl"))
    clips, tokens = ("z", "yh", "core"), ("x", "yl")
    rows = P(clips, tokens, None)
    return jax.shard_map(
        local,
        mesh=inner,
        in_specs=(rows,) * 6 + (P(clips, tokens), P(clips, None, None, None)),
        out_specs=(rows, rows, rows),
        check_vma=False,
    )
```

```python
import functools
import math

import jax
import jax.numpy as jnp
from jax import lax
from jax.experimental import pallas as pl
from jax.experimental.pallas import tpu as pltpu
from jax.sharding import Mesh, PartitionSpec as P


BF = jnp.bfloat16
F32 = jnp.float32
HD = 128
TILE = 64
SCALE = HD**-0.5
LOG2E = math.log2(math.e)

QA, KA, VA, OA, KC, VC, QC, OC, NR = 0, 128, 256, 384, 512, 640, 768, 832, 896
IN_ROWS = 912
SLAB = 768
GRANT = 16 << 20
WHOLE_GRANT = 62 << 20
WIDE_GRANT = 52 << 20
MID = 192
GQA, GKA, GVA, GKC, GVC, GQC = 0, 128, 256, 384, 512, 640
OUT_ROWS = 704

NT_DIMS = (((1,), (1,)), ((), ()))
NN_DIMS = (((1,), (0,)), ((), ()))
TN_DIMS = (((0,), (0,)), ((), ()))


def dot(a, b, dims):
    return lax.dot_general(a, b, dims, preferred_element_type=F32)


def load(sources, targets, sems):
    copies = [pltpu.make_async_copy(a, b, sems.at[n]) for n, (a, b) in enumerate(zip(sources, targets, strict=True))]
    for copy in copies:
        copy.start()
    for copy in copies:
        copy.wait()


def pack_kernel(me_ref, q_hbm, k_hbm, v_hbm, o_hbm, n_hbm, g_hbm, *refs):
    out_refs = refs[:8]
    q_ref, k_ref, v_ref, o_ref, n_ref, g_ref, sems = refs[8:]
    load((q_hbm, k_hbm, v_hbm, o_hbm, n_hbm, g_hbm), (q_ref, k_ref, v_ref, o_ref, n_ref, g_ref), sems)
    for d, out_ref in enumerate(out_refs):
        to = jnp.bitwise_xor(me_ref[0], d)
        x, y = to // 2, to % 2
        base = 0 if d % 2 else SLAB
        own = pl.ds(pl.multiple_of(HD * (3 * x + y), HD), HD)
        shared = pl.ds(pl.multiple_of(HD * (3 * x + 2), HD), HD)
        half = pl.ds(pl.multiple_of(TILE * y, TILE), TILE)
        if base:
            for e in range(6):
                columns = pl.ds(pl.multiple_of(768 * x + 128 * e, 128), 128)
                out_ref[128 * e : 128 * (e + 1)] = g_ref[:, columns]
        for ref, at in ((q_ref, QA), (k_ref, KA), (v_ref, VA), (o_ref, OA)):
            out_ref[base + at : base + at + 128] = ref[:, own]
        for ref, at in ((k_ref, KC), (v_ref, VC)):
            out_ref[base + at : base + at + 128] = ref[:, shared]
        for ref, at in ((q_ref, QC), (o_ref, OC)):
            out_ref[base + at : base + at + 64] = ref[half, shared]
        line = lax.broadcasted_iota(jnp.int32, (16, 12), 0)
        head = lax.broadcasted_iota(jnp.int32, (16, 12), 1)
        wanted = jnp.where(line == 0, 3 * x + y, 3 * x + 2)
        pick = jnp.where((head == wanted) & (line < 2), 1.0, 0.0).astype(BF)
        out_ref[base + NR : base + IN_ROWS] = dot(pick, n_ref[...], NN_DIMS).astype(BF)


def pack(me, q, k, v, o, norms, out_grad):
    whole = pl.BlockSpec(memory_space=pltpu.VMEM)
    return pl.pallas_call(
        pack_kernel,
        in_specs=[pl.BlockSpec(memory_space=pltpu.SMEM)] + [pl.BlockSpec(memory_space=pl.ANY)] * 6,
        out_specs=(whole,) * 8,
        out_shape=tuple(jax.ShapeDtypeStruct((IN_ROWS + (0 if d % 2 else SLAB), 128), BF) for d in range(8)),
        scratch_shapes=[
            *[pltpu.VMEM((128, 1536), BF)] * 4,
            pltpu.VMEM((12, 128), BF),
            pltpu.VMEM((128, 3072), BF),
            pltpu.SemaphoreType.DMA((6,)),
        ],
        compiler_params=pltpu.CompilerParams(vmem_limit_bytes=WHOLE_GRANT),
        name="pack",
    )(me, q, k, v, o, norms, out_grad)


def project_kernel(where_ref, own_ref, other_ref, g0_ref, g1_ref, g2_ref, g3_ref, out_ref, w_ref, g_ref):
    @pl.when(pl.program_id(0) == 0)
    def _():
        for e, ref in enumerate((g0_ref, g1_ref, g2_ref, g3_ref)):
            source = jnp.bitwise_xor(where_ref[1], e)
            for n in range(6):
                g_ref[source, :, 128 * n : 128 * (n + 1)] = ref[128 * n : 128 * (n + 1)]

    mine = where_ref[0] == 0
    for z in range(4):
        for yh in range(2):
            for yl in range(2):
                a = own_ref[yh, yl, z]
                b = other_ref[yh, yl, z]
                for c in range(2):
                    row = 24 * (4 * z + 2 * yh + c)
                    piece = jnp.where(mine, a, b) if c == 0 else jnp.where(mine, b, a)
                    w_ref[row : row + 24, 384 * yl : 384 * (yl + 1)] = piece
    g = g_ref[...].reshape(512, 768)
    part = dot(g, w_ref[...], NT_DIMS).astype(BF)
    for x in range(4):
        rows = slice(128 * x, 128 * (x + 1))
        for j in range(2):
            base = MID * x
            out_ref[j, base : base + 128] = part[rows, HD * j : HD * (j + 1)]
            out_ref[j, base + 128 : base + MID] = part[128 * x + 64 * j : 128 * x + 64 * (j + 1), 2 * HD :]


def project(where, own, other, slabs):
    shard = pl.BlockSpec((2, 2, 4, 24, 384), lambda i: (0, 0, i, 0, 0))
    slab = pl.BlockSpec((SLAB, 128), lambda i: (0, 0))
    return pl.pallas_call(
        project_kernel,
        grid=(4,),
        in_specs=[pl.BlockSpec(memory_space=pltpu.SMEM), shard, shard] + [slab] * 4,
        out_specs=pl.BlockSpec((2, 4 * MID, 128), lambda i: (i, 0, 0)),
        out_shape=jax.ShapeDtypeStruct((8, 4 * MID, 128), BF),
        scratch_shapes=[pltpu.VMEM((384, 768), BF), pltpu.VMEM((4, 128, 768), BF)],
        compiler_params=pltpu.CompilerParams(vmem_limit_bytes=GRANT),
        name="project",
    )(where, own, other, *slabs)


KEYS = 1024
CHUNK = 256
BLOCKS = 6


def score_unit(in_ref, mask_ref, prob_ref, copies, per, rows, block0, norm_row):
    q0, k0 = rows
    group = 256 // per
    for b in range(8 // group):
        q = jnp.concatenate([in_ref[s, q0 : q0 + per] for s in range(group * b, group * (b + 1))], axis=0)
        norm = norm_row(b)
        for n in range(KEYS // CHUNK):
            k = in_ref[2 * n : 2 * n + 2, k0 : k0 + 128].reshape(CHUNK, HD)
            prob = jnp.exp2(dot(k, q, NT_DIMS) * (SCALE * LOG2E) - norm)
            allowed = mask_ref[4 * n : 4 * (n + 1), 256 * b : 256 * (b + 1)]
            prob = (prob.reshape(4, TILE, 256) * allowed[:, None, :]).reshape(CHUNK, 256)
            prob_ref[block0 + b, CHUNK * n : CHUNK * (n + 1)] = prob
        copies[block0 + b].start()


def score_kernel(me_ref, *refs):
    sent_refs = refs[:8]
    mask_a_hbm, mask_c_hbm, in_ref, prob_hbm, prob_ref, mask_a_ref, mask_c_ref, sems, prob_sems = refs[8:]
    sources = [ref if d % 2 else ref.at[pl.ds(SLAB, IN_ROWS)] for d, ref in enumerate(sent_refs)]
    targets = [in_ref.at[jnp.bitwise_xor(me_ref[0], d)] for d in range(8)]
    load((*sources, mask_a_hbm, mask_c_hbm), (*targets, mask_a_ref, mask_c_ref), sems)
    second = me_ref[0] % 2 == 1

    def norm_a(b):
        parts = [in_ref[s, NR : NR + 16].astype(F32)[0:1] for s in (2 * b, 2 * b + 1)]
        return jnp.concatenate(parts, axis=1) * LOG2E

    def norm_c(b):
        parts = []
        for s in range(4 * b, 4 * b + 4):
            row = in_ref[s, NR : NR + 16].astype(F32)[1:2]
            parts.append(jnp.where(second, row[:, 64:], row[:, :64]))
        return jnp.concatenate(parts, axis=1) * LOG2E

    copies = [pltpu.make_async_copy(prob_ref.at[b], prob_hbm.at[b], prob_sems.at[b]) for b in range(BLOCKS)]
    score_unit(in_ref, mask_a_ref, prob_ref, copies, 128, (QA, KA), 0, norm_a)
    score_unit(in_ref, mask_c_ref, prob_ref, copies, 64, (QC, KC), 4, norm_c)
    for copy in copies:
        copy.wait()


def score(me, arrived, mask_a, mask_c):
    whole = pl.BlockSpec(memory_space=pltpu.VMEM)
    return pl.pallas_call(
        score_kernel,
        in_specs=[pl.BlockSpec(memory_space=pltpu.SMEM)] + [pl.BlockSpec(memory_space=pl.ANY)] * 10,
        out_specs=(whole, pl.BlockSpec(memory_space=pl.ANY)),
        out_shape=(
            jax.ShapeDtypeStruct((8, IN_ROWS, 128), BF),
            jax.ShapeDtypeStruct((BLOCKS, KEYS, 256), F32),
        ),
        scratch_shapes=[
            pltpu.VMEM((BLOCKS, KEYS, 256), F32),
            pltpu.VMEM((16, 1024), F32),
            pltpu.VMEM((16, 512), F32),
            pltpu.SemaphoreType.DMA((10,)),
            pltpu.SemaphoreType.DMA((BLOCKS,)),
        ],
        compiler_params=pltpu.CompilerParams(vmem_limit_bytes=WIDE_GRANT),
        name="score",
    )(me, *arrived, mask_a, mask_c)


def attend_unit(in_ref, prob_ref, copies, mid_ref, out_ref, dk_ref, dv_ref, per, rows, block0, outs):
    q0, o0, k0, v0, m0 = rows
    gq0, gk0, gv0 = outs
    group = 256 // per
    for b in range(8 // group):
        sources = range(group * b, group * (b + 1))
        q = jnp.concatenate([in_ref[s, q0 : q0 + per] for s in sources], axis=0)
        o = jnp.concatenate([in_ref[s, o0 : o0 + per] for s in sources], axis=0)
        pieces = []
        for s in sources:
            base = MID * (s // 2) + m0
            total = mid_ref[s % 2, base : base + per].astype(F32)
            for x in range(1, 4):
                total = total + mid_ref[2 * x + s % 2, base : base + per].astype(F32)
            pieces.append(total.astype(BF))
        g = jnp.concatenate(pieces, axis=0)
        product = g.astype(F32) * o.astype(F32)
        dots = lax.dot_general(
            jnp.ones((8, 128), F32), product, NT_DIMS, precision=lax.Precision.HIGHEST, preferred_element_type=F32
        )[0:1]
        dots = dots.astype(BF).astype(F32)
        dq = jnp.zeros((HD, 256), F32)
        copies[block0 + b].wait()
        for n in range(KEYS // CHUNK):
            src = slice(2 * n, 2 * n + 2)
            at = slice(CHUNK * n, CHUNK * (n + 1))
            k = in_ref[src, k0 : k0 + 128].reshape(CHUNK, HD)
            v = in_ref[src, v0 : v0 + 128].reshape(CHUNK, HD)
            prob = prob_ref[block0 + b, at]
            score_grad = (prob * (dot(v, g, NT_DIMS) - dots)).astype(BF)
            dv = dot(prob.astype(BF), g, NN_DIMS)
            dk = dot(score_grad, q, NN_DIMS)
            if b == 0:
                dv_ref[at] = dv
                dk_ref[at] = dk
            else:
                dv_ref[at] += dv
                dk_ref[at] += dk
            dq = dq + dot(k, score_grad, TN_DIMS)
        dq = (dq.T * SCALE).astype(BF)
        for e, s in enumerate(sources):
            out_ref[s, gq0 : gq0 + per] = dq[per * e : per * (e + 1)]
    for s in range(8):
        at = slice(128 * s, 128 * (s + 1))
        out_ref[s, gk0 : gk0 + 128] = (dk_ref[at] * SCALE).astype(BF)
        out_ref[s, gv0 : gv0 + 128] = dv_ref[at].astype(BF)


def attend_kernel(in_ref, prob_hbm, mid_ref, out_ref, prob_ref, dk_ref, dv_ref, sems):
    copies = [pltpu.make_async_copy(prob_hbm.at[b], prob_ref.at[b], sems.at[b]) for b in range(BLOCKS)]
    for copy in copies:
        copy.start()
    refs = (in_ref, prob_ref, copies, mid_ref, out_ref, dk_ref, dv_ref)
    attend_unit(*refs, 128, (QA, OA, KA, VA, 0), 0, (GQA, GKA, GVA))
    attend_unit(*refs, 64, (QC, OC, KC, VC, 128), 4, (GQC, GKC, GVC))


def attend(inputs, prob, partial):
    whole = pl.BlockSpec(memory_space=pltpu.VMEM)
    return pl.pallas_call(
        attend_kernel,
        in_specs=[whole, pl.BlockSpec(memory_space=pl.ANY), whole],
        out_specs=whole,
        out_shape=jax.ShapeDtypeStruct((8, OUT_ROWS, 128), BF),
        scratch_shapes=[
            pltpu.VMEM((BLOCKS, KEYS, 256), F32),
            pltpu.VMEM((KEYS, 128), F32),
            pltpu.VMEM((KEYS, 128), F32),
            pltpu.SemaphoreType.DMA((BLOCKS,)),
        ],
        compiler_params=pltpu.CompilerParams(vmem_limit_bytes=WIDE_GRANT),
        name="attend",
    )(inputs, prob, partial)


def merge_kernel(in_ref, gq_ref, gk_ref, gv_ref):
    for j in range(2):
        own = slice(HD * j, HD * (j + 1))
        gq_ref[0, :, own] = in_ref[j, GQA : GQA + 128]
        gk_ref[0, :, own] = in_ref[j, GKA : GKA + 128]
        gv_ref[0, :, own] = in_ref[j, GVA : GVA + 128]
        gq_ref[0, TILE * j : TILE * (j + 1), 2 * HD :] = in_ref[j, GQC : GQC + 64]
    for ref, at in ((gk_ref, GKC), (gv_ref, GVC)):
        total = in_ref[0, at : at + 128].astype(F32) + in_ref[1, at : at + 128].astype(F32)
        ref[0, :, 2 * HD :] = total.astype(BF)


def merge(arrived):
    out = pl.BlockSpec((1, 128, 3 * HD), lambda i: (0, 0, i))
    shape = jax.ShapeDtypeStruct((1, 128, 1536), BF)
    return pl.pallas_call(
        merge_kernel,
        grid=(4,),
        in_specs=[pl.BlockSpec((2, OUT_ROWS, 128), lambda i: (i, 0, 0))],
        out_specs=(out, out, out),
        out_shape=(shape, shape, shape),
        compiler_params=pltpu.CompilerParams(vmem_limit_bytes=GRANT),
        name="merge",
    )(arrived)


def exchange(array, axes):
    return lax.all_to_all(array, axes, split_axis=0, concat_axis=0, tiled=True)


def spread(array, axes, count):
    return exchange(jnp.broadcast_to(array[None], (count,) + array.shape), axes)


def gather_weight(proj_weight):
    own = spread(proj_weight, "z", 16)
    own = spread(own, ("yh", "yl"), 4).reshape(2, 2, 16, 24, 384)
    other = lax.ppermute(own, "core", [(0, 1), (1, 0)])
    return own, other


def mask_kernel(shared, where_ref, table_ref, out_ref):
    x, y = where_ref[0] // 2, where_ref[0] % 2
    tile = lax.broadcasted_iota(jnp.int32, out_ref.shape, 0)
    group = lax.broadcasted_iota(jnp.int32, out_ref.shape, 1) // TILE
    of_lane = 2 * group + y if shared else group
    head = 3 * x + 2 if shared else 3 * x + y
    out_ref[...] = dot(table_ref[0, head].astype(F32), jnp.where(tile == of_lane, 1.0, 0.0), TN_DIMS)


def mask_rows(me, tile_mask, shared):
    whole = pl.BlockSpec(memory_space=pltpu.VMEM)
    return pl.pallas_call(
        functools.partial(mask_kernel, shared),
        in_specs=[pl.BlockSpec(memory_space=pltpu.SMEM), whole],
        out_specs=whole,
        out_shape=jax.ShapeDtypeStruct((16, 512 if shared else 1024), F32),
        compiler_params=pltpu.CompilerParams(vmem_limit_bytes=GRANT),
        name="mask",
    )(me, tile_mask)


def swap(array, d):
    return lax.ppermute(array, ("x", "yl"), [(s, s ^ d) for s in range(8)])


def after_weight(q, k, v, o, log_norm, out_grad, own, other, core, tile_mask):
    x, y = lax.axis_index("x"), lax.axis_index("yl")
    me = (2 * x + y).reshape(1)
    where = jnp.stack([core, x])
    sent = pack(me, q[0], k[0], v[0], o[0], log_norm[0].T, out_grad[0])
    arrived = [sent[d] if d == 0 else swap(sent[d], d) for d in range(8)]
    part = project(where, own, other, arrived[::2])
    partial = exchange(part, ("x", "yl"))
    mask_a, mask_c = mask_rows(me, tile_mask, False), mask_rows(me, tile_mask, True)
    inputs, prob = score(me, arrived, mask_a, mask_c)
    result = exchange(attend(inputs, prob, partial), ("x", "yl"))
    return merge(result)


def local(queries, key_states, value_states, attn_out, log_norm, out_grad, proj_weight, tile_mask):
    own, other = gather_weight(proj_weight)
    return after_weight(
        queries,
        key_states,
        value_states,
        attn_out,
        log_norm,
        out_grad,
        own,
        other,
        lax.axis_index("core"),
        tile_mask,
    )


def solution(mesh):
    inner = Mesh(mesh.devices.reshape(16, 2, 2, 4, 2), ("z", "yh", "core", "x", "yl"))
    clips, tokens = ("z", "yh", "core"), ("x", "yl")
    rows = P(clips, tokens, None)
    return jax.shard_map(
        local,
        mesh=inner,
        in_specs=(rows,) * 6 + (P(clips, tokens), P(clips, None, None, None)),
        out_specs=(rows, rows, rows),
        check_vma=False,
    )
```

```python
import functools
import math

import jax
import jax.numpy as jnp
from jax import lax
from jax.experimental import pallas as pl
from jax.experimental.pallas import tpu as pltpu
from jax.sharding import Mesh, PartitionSpec as P


BF = jnp.bfloat16
F32 = jnp.float32
HD = 128
TILE = 64
SCALE = HD**-0.5
LOG2E = math.log2(math.e)

QA, KA, VA, OA, KC, VC, QC, OC, NR = 0, 128, 256, 384, 512, 640, 768, 832, 896
IN_ROWS = 912
SLAB = 768
GRANT = 16 << 20
WHOLE_GRANT = 62 << 20
MID = 192
GQA, GKA, GVA, GKC, GVC, GQC = 0, 128, 256, 384, 512, 640
OUT_ROWS = 704

NT_DIMS = (((1,), (1,)), ((), ()))
NN_DIMS = (((1,), (0,)), ((), ()))
TN_DIMS = (((0,), (0,)), ((), ()))


def dot(a, b, dims):
    return lax.dot_general(a, b, dims, preferred_element_type=F32)


def start(sources, targets, sems):
    copies = [pltpu.make_async_copy(a, b, sems.at[n]) for n, (a, b) in enumerate(zip(sources, targets, strict=True))]
    for copy in copies:
        copy.start()
    return copies


def pack_kernel(me_ref, q_hbm, k_hbm, v_hbm, o_hbm, n_hbm, g_hbm, *refs):
    out_refs = refs[:8]
    q_ref, k_ref, v_ref, o_ref, n_ref, g_ref, sems = refs[8:]
    for copy in start((q_hbm, k_hbm, v_hbm, o_hbm, n_hbm, g_hbm), (q_ref, k_ref, v_ref, o_ref, n_ref, g_ref), sems):
        copy.wait()
    for d, out_ref in enumerate(out_refs):
        to = jnp.bitwise_xor(me_ref[0], d)
        x, y = to // 2, to % 2
        base = 0 if d % 2 else SLAB
        own = pl.ds(pl.multiple_of(HD * (3 * x + y), HD), HD)
        shared = pl.ds(pl.multiple_of(HD * (3 * x + 2), HD), HD)
        half = pl.ds(pl.multiple_of(TILE * y, TILE), TILE)
        if base:
            for e in range(6):
                columns = pl.ds(pl.multiple_of(768 * x + 128 * e, 128), 128)
                out_ref[128 * e : 128 * (e + 1)] = g_ref[:, columns]
        for ref, at in ((q_ref, QA), (k_ref, KA), (v_ref, VA), (o_ref, OA)):
            out_ref[base + at : base + at + 128] = ref[:, own]
        for ref, at in ((k_ref, KC), (v_ref, VC)):
            out_ref[base + at : base + at + 128] = ref[:, shared]
        for ref, at in ((q_ref, QC), (o_ref, OC)):
            out_ref[base + at : base + at + 64] = ref[half, shared]
        line = lax.broadcasted_iota(jnp.int32, (16, 12), 0)
        head = lax.broadcasted_iota(jnp.int32, (16, 12), 1)
        wanted = jnp.where(line == 0, 3 * x + y, 3 * x + 2)
        pick = jnp.where((head == wanted) & (line < 2), 1.0, 0.0).astype(BF)
        out_ref[base + NR : base + IN_ROWS] = dot(pick, n_ref[...], NN_DIMS).astype(BF)


def pack(me, q, k, v, o, norms, out_grad):
    whole = pl.BlockSpec(memory_space=pltpu.VMEM)
    return pl.pallas_call(
        pack_kernel,
        in_specs=[pl.BlockSpec(memory_space=pltpu.SMEM)] + [pl.BlockSpec(memory_space=pl.ANY)] * 6,
        out_specs=(whole,) * 8,
        out_shape=tuple(jax.ShapeDtypeStruct((IN_ROWS + (0 if d % 2 else SLAB), 128), BF) for d in range(8)),
        scratch_shapes=[
            *[pltpu.VMEM((128, 1536), BF)] * 4,
            pltpu.VMEM((12, 128), BF),
            pltpu.VMEM((128, 3072), BF),
            pltpu.SemaphoreType.DMA((6,)),
        ],
        compiler_params=pltpu.CompilerParams(vmem_limit_bytes=WHOLE_GRANT),
        name="pack",
    )(me, q, k, v, o, norms, out_grad)


def project_kernel(where_ref, own_ref, other_ref, g0_ref, g1_ref, g2_ref, g3_ref, out_ref, w_ref, g_ref):
    @pl.when(pl.program_id(0) == 0)
    def _():
        for e, ref in enumerate((g0_ref, g1_ref, g2_ref, g3_ref)):
            source = jnp.bitwise_xor(where_ref[1], e)
            for n in range(6):
                g_ref[source, :, 128 * n : 128 * (n + 1)] = ref[128 * n : 128 * (n + 1)]

    mine = where_ref[0] == 0
    for z in range(4):
        for yh in range(2):
            for yl in range(2):
                a = own_ref[yh, yl, z]
                b = other_ref[yh, yl, z]
                for c in range(2):
                    row = 24 * (4 * z + 2 * yh + c)
                    piece = jnp.where(mine, a, b) if c == 0 else jnp.where(mine, b, a)
                    w_ref[row : row + 24, 384 * yl : 384 * (yl + 1)] = piece
    g = g_ref[...].reshape(512, 768)
    part = dot(g, w_ref[...], NT_DIMS).astype(BF)
    for x in range(4):
        rows = slice(128 * x, 128 * (x + 1))
        for j in range(2):
            base = MID * x
            out_ref[j, base : base + 128] = part[rows, HD * j : HD * (j + 1)]
            out_ref[j, base + 128 : base + MID] = part[128 * x + 64 * j : 128 * x + 64 * (j + 1), 2 * HD :]


def project(where, own, other, slabs):
    shard = pl.BlockSpec((2, 2, 4, 24, 384), lambda i: (0, 0, i, 0, 0))
    slab = pl.BlockSpec((SLAB, 128), lambda i: (0, 0))
    return pl.pallas_call(
        project_kernel,
        grid=(4,),
        in_specs=[pl.BlockSpec(memory_space=pltpu.SMEM), shard, shard] + [slab] * 4,
        out_specs=pl.BlockSpec((2, 4 * MID, 128), lambda i: (i, 0, 0)),
        out_shape=jax.ShapeDtypeStruct((8, 4 * MID, 128), BF),
        scratch_shapes=[pltpu.VMEM((384, 768), BF), pltpu.VMEM((4, 128, 768), BF)],
        compiler_params=pltpu.CompilerParams(vmem_limit_bytes=GRANT),
        name="project",
    )(where, own, other, *slabs)


def attend_unit(in_ref, g_ref, mask_ref, out_ref, dk_ref, dv_ref, per, rows, norm_row, outs):
    q0, o0, k0, v0, g0 = rows
    gq0, gk0, gv0 = outs
    group = 256 // per
    keys = 1024
    chunk = 256
    for b in range(8 // group):
        sources = range(group * b, group * (b + 1))
        q = jnp.concatenate([in_ref[s, q0 : q0 + per] for s in sources], axis=0)
        o = jnp.concatenate([in_ref[s, o0 : o0 + per] for s in sources], axis=0)
        g = g_ref[g0 + 256 * b : g0 + 256 * (b + 1)]
        product = g.astype(F32) * o.astype(F32)
        dots = lax.dot_general(
            jnp.ones((8, 128), F32), product, NT_DIMS, precision=lax.Precision.HIGHEST, preferred_element_type=F32
        )[0:1]
        dots = dots.astype(BF).astype(F32)
        norm = norm_row(b)
        dq = jnp.zeros((HD, 256), F32)
        for n in range(keys // chunk):
            src = slice(2 * n, 2 * n + 2)
            k = in_ref[src, k0 : k0 + 128].reshape(chunk, HD)
            v = in_ref[src, v0 : v0 + 128].reshape(chunk, HD)
            scores = dot(k, q, NT_DIMS)
            prob = jnp.exp2(scores * (SCALE * LOG2E) - norm)
            allowed = mask_ref[4 * n : 4 * (n + 1), 256 * b : 256 * (b + 1)]
            prob = (prob.reshape(4, TILE, 256) * allowed[:, None, :]).reshape(chunk, 256)
            score_grad = prob * (dot(v, g, NT_DIMS) - dots)
            prob = prob.astype(BF)
            score_grad = score_grad.astype(BF)
            dv = dot(prob, g, NN_DIMS)
            dk = dot(score_grad, q, NN_DIMS)
            at = slice(chunk * n, chunk * (n + 1))
            if b == 0:
                dv_ref[at] = dv
                dk_ref[at] = dk
            else:
                dv_ref[at] += dv
                dk_ref[at] += dk
            dq = dq + dot(k, score_grad, TN_DIMS)
        dq = (dq.T * SCALE).astype(BF)
        for e, s in enumerate(sources):
            out_ref[s, gq0 : gq0 + per] = dq[per * e : per * (e + 1)]
    for s in range(8):
        at = slice(128 * s, 128 * (s + 1))
        out_ref[s, gk0 : gk0 + 128] = (dk_ref[at] * SCALE).astype(BF)
        out_ref[s, gv0 : gv0 + 128] = dv_ref[at].astype(BF)


def attend_kernel(me_ref, *refs):
    sent_refs = refs[:8]
    mid_ref, mask_a_hbm, mask_c_hbm, out_ref, in_ref, g_ref, dk_ref, dv_ref, mask_a_ref, mask_c_ref, sems = refs[8:]
    sources = [ref if d % 2 else ref.at[pl.ds(SLAB, IN_ROWS)] for d, ref in enumerate(sent_refs)]
    targets = [in_ref.at[jnp.bitwise_xor(me_ref[0], d)] for d in range(8)]
    copies = start((*sources, mask_a_hbm, mask_c_hbm), (*targets, mask_a_ref, mask_c_ref), sems)
    for per, m0, g0 in ((128, 0, 0), (64, 128, 1024)):
        for s in range(8):
            piece = slice(MID * (s // 2) + m0, MID * (s // 2) + m0 + per)
            total = mid_ref[s % 2, piece].astype(F32)
            for x in range(1, 4):
                total = total + mid_ref[2 * x + s % 2, piece].astype(F32)
            g_ref[g0 + per * s : g0 + per * (s + 1)] = total.astype(BF)
    for copy in copies:
        copy.wait()
    second = me_ref[0] % 2 == 1

    def norm_a(b):
        parts = [in_ref[s, NR : NR + 16].astype(F32)[0:1] for s in (2 * b, 2 * b + 1)]
        return jnp.concatenate(parts, axis=1) * LOG2E

    def norm_c(b):
        parts = []
        for s in range(4 * b, 4 * b + 4):
            row = in_ref[s, NR : NR + 16].astype(F32)[1:2]
            parts.append(jnp.where(second, row[:, 64:], row[:, :64]))
        return jnp.concatenate(parts, axis=1) * LOG2E

    attend_unit(
        in_ref, g_ref, mask_a_ref, out_ref, dk_ref, dv_ref, 128, (QA, OA, KA, VA, 0), norm_a, (GQA, GKA, GVA)
    )
    attend_unit(
        in_ref, g_ref, mask_c_ref, out_ref, dk_ref, dv_ref, 64, (QC, OC, KC, VC, 1024), norm_c, (GQC, GKC, GVC)
    )


def attend(me, arrived, partial, mask_a, mask_c):
    whole = pl.BlockSpec(memory_space=pltpu.VMEM)
    return pl.pallas_call(
        attend_kernel,
        in_specs=[pl.BlockSpec(memory_space=pltpu.SMEM)]
        + [pl.BlockSpec(memory_space=pl.ANY)] * 8
        + [whole]
        + [pl.BlockSpec(memory_space=pl.ANY)] * 2,
        out_specs=whole,
        out_shape=jax.ShapeDtypeStruct((8, OUT_ROWS, 128), BF),
        scratch_shapes=[
            pltpu.VMEM((8, IN_ROWS, 128), BF),
            pltpu.VMEM((1536, 128), BF),
            pltpu.VMEM((1024, 128), F32),
            pltpu.VMEM((1024, 128), F32),
            pltpu.VMEM((16, 1024), F32),
            pltpu.VMEM((16, 512), F32),
            pltpu.SemaphoreType.DMA((10,)),
        ],
        compiler_params=pltpu.CompilerParams(vmem_limit_bytes=GRANT),
        name="attend",
    )(me, *arrived, partial, mask_a, mask_c)


def merge_kernel(in_ref, gq_ref, gk_ref, gv_ref):
    for j in range(2):
        own = slice(HD * j, HD * (j + 1))
        gq_ref[0, :, own] = in_ref[j, GQA : GQA + 128]
        gk_ref[0, :, own] = in_ref[j, GKA : GKA + 128]
        gv_ref[0, :, own] = in_ref[j, GVA : GVA + 128]
        gq_ref[0, TILE * j : TILE * (j + 1), 2 * HD :] = in_ref[j, GQC : GQC + 64]
    for ref, at in ((gk_ref, GKC), (gv_ref, GVC)):
        total = in_ref[0, at : at + 128].astype(F32) + in_ref[1, at : at + 128].astype(F32)
        ref[0, :, 2 * HD :] = total.astype(BF)


def merge(arrived):
    out = pl.BlockSpec((1, 128, 3 * HD), lambda i: (0, 0, i))
    shape = jax.ShapeDtypeStruct((1, 128, 1536), BF)
    return pl.pallas_call(
        merge_kernel,
        grid=(4,),
        in_specs=[pl.BlockSpec((2, OUT_ROWS, 128), lambda i: (i, 0, 0))],
        out_specs=(out, out, out),
        out_shape=(shape, shape, shape),
        compiler_params=pltpu.CompilerParams(vmem_limit_bytes=GRANT),
        name="merge",
    )(arrived)


def exchange(array, axes):
    return lax.all_to_all(array, axes, split_axis=0, concat_axis=0, tiled=True)


def spread(array, axes, count):
    return exchange(jnp.broadcast_to(array[None], (count,) + array.shape), axes)


def gather_weight(proj_weight):
    own = spread(proj_weight, "z", 16)
    own = spread(own, ("yh", "yl"), 4).reshape(2, 2, 16, 24, 384)
    other = lax.ppermute(own, "core", [(0, 1), (1, 0)])
    return own, other


def mask_kernel(shared, where_ref, table_ref, out_ref):
    x, y = where_ref[0] // 2, where_ref[0] % 2
    tile = lax.broadcasted_iota(jnp.int32, out_ref.shape, 0)
    group = lax.broadcasted_iota(jnp.int32, out_ref.shape, 1) // TILE
    of_lane = 2 * group + y if shared else group
    head = 3 * x + 2 if shared else 3 * x + y
    out_ref[...] = dot(table_ref[0, head].astype(F32), jnp.where(tile == of_lane, 1.0, 0.0), TN_DIMS)


def mask_rows(me, tile_mask, shared):
    whole = pl.BlockSpec(memory_space=pltpu.VMEM)
    return pl.pallas_call(
        functools.partial(mask_kernel, shared),
        in_specs=[pl.BlockSpec(memory_space=pltpu.SMEM), whole],
        out_specs=whole,
        out_shape=jax.ShapeDtypeStruct((16, 512 if shared else 1024), F32),
        compiler_params=pltpu.CompilerParams(vmem_limit_bytes=GRANT),
        name="mask",
    )(me, tile_mask)


def swap(array, d):
    return lax.ppermute(array, ("x", "yl"), [(s, s ^ d) for s in range(8)])


def after_weight(q, k, v, o, log_norm, out_grad, own, other, core, tile_mask):
    x, y = lax.axis_index("x"), lax.axis_index("yl")
    me = (2 * x + y).reshape(1)
    where = jnp.stack([core, x])
    sent = pack(me, q[0], k[0], v[0], o[0], log_norm[0].T, out_grad[0])
    arrived = [sent[d] if d in (0, 4, 5) else swap(sent[d], d) for d in range(8)]
    arrived[4] = swap(swap(sent[4], 2), 6)
    arrived[5] = swap(swap(sent[5], 3), 6)
    partial = exchange(project(where, own, other, arrived[::2]), ("x", "yl"))
    mask_a, mask_c = mask_rows(me, tile_mask, False), mask_rows(me, tile_mask, True)
    result = exchange(attend(me, arrived, partial, mask_a, mask_c), ("x", "yl"))
    return merge(result)


def local(queries, key_states, value_states, attn_out, log_norm, out_grad, proj_weight, tile_mask):
    own, other = gather_weight(proj_weight)
    return after_weight(
        queries,
        key_states,
        value_states,
        attn_out,
        log_norm,
        out_grad,
        own,
        other,
        lax.axis_index("core"),
        tile_mask,
    )


def solution(mesh):
    inner = Mesh(mesh.devices.reshape(16, 2, 2, 4, 2), ("z", "yh", "core", "x", "yl"))
    clips, tokens = ("z", "yh", "core"), ("x", "yl")
    rows = P(clips, tokens, None)
    return jax.shard_map(
        local,
        mesh=inner,
        in_specs=(rows,) * 6 + (P(clips, tokens), P(clips, None, None, None)),
        out_specs=(rows, rows, rows),
        check_vma=False,
    )
```

```python
import functools
import math

import jax
import jax.numpy as jnp
from jax import lax
from jax.experimental import pallas as pl
from jax.experimental.pallas import tpu as pltpu
from jax.sharding import Mesh, PartitionSpec as P


BF = jnp.bfloat16
F32 = jnp.float32
HD = 128
TILE = 64
SCALE = HD**-0.5
LOG2E = math.log2(math.e)

QA, KA, VA, OA, KC, VC, QC, OC, NR = 0, 128, 256, 384, 512, 640, 768, 832, 896
IN_ROWS = 912
SLAB = 768
GRANT = 16 << 20
WHOLE_GRANT = 62 << 20
GQA, GKA, GVA, GKC, GVC, GQC = 0, 128, 256, 384, 512, 640
OUT_ROWS = 704

NT_DIMS = (((1,), (1,)), ((), ()))
NN_DIMS = (((1,), (0,)), ((), ()))
TN_DIMS = (((0,), (0,)), ((), ()))


def dot(a, b, dims):
    return lax.dot_general(a, b, dims, preferred_element_type=F32)


def start(sources, targets, sems):
    copies = [pltpu.make_async_copy(a, b, sems.at[n]) for n, (a, b) in enumerate(zip(sources, targets, strict=True))]
    for copy in copies:
        copy.start()
    return copies


def pack_kernel(me_ref, q_hbm, k_hbm, v_hbm, o_hbm, n_hbm, g_hbm, *refs):
    out_refs = refs[:8]
    q_ref, k_ref, v_ref, o_ref, n_ref, g_ref, sems = refs[8:]
    for copy in start((q_hbm, k_hbm, v_hbm, o_hbm, n_hbm, g_hbm), (q_ref, k_ref, v_ref, o_ref, n_ref, g_ref), sems):
        copy.wait()
    for d, out_ref in enumerate(out_refs):
        to = jnp.bitwise_xor(me_ref[0], d)
        x, y = to // 2, to % 2
        base = 0 if d % 2 else SLAB
        own = pl.ds(pl.multiple_of(HD * (3 * x + y), HD), HD)
        shared = pl.ds(pl.multiple_of(HD * (3 * x + 2), HD), HD)
        half = pl.ds(pl.multiple_of(TILE * y, TILE), TILE)
        if base:
            for e in range(6):
                columns = pl.ds(pl.multiple_of(768 * x + 128 * e, 128), 128)
                out_ref[128 * e : 128 * (e + 1)] = g_ref[:, columns]
        for ref, at in ((q_ref, QA), (k_ref, KA), (v_ref, VA), (o_ref, OA)):
            out_ref[base + at : base + at + 128] = ref[:, own]
        for ref, at in ((k_ref, KC), (v_ref, VC)):
            out_ref[base + at : base + at + 128] = ref[:, shared]
        for ref, at in ((q_ref, QC), (o_ref, OC)):
            out_ref[base + at : base + at + 64] = ref[half, shared]
        line = lax.broadcasted_iota(jnp.int32, (16, 12), 0)
        head = lax.broadcasted_iota(jnp.int32, (16, 12), 1)
        wanted = jnp.where(line == 0, 3 * x + y, 3 * x + 2)
        pick = jnp.where((head == wanted) & (line < 2), 1.0, 0.0).astype(BF)
        out_ref[base + NR : base + IN_ROWS] = dot(pick, n_ref[...], NN_DIMS).astype(BF)


def pack(me, q, k, v, o, norms, out_grad):
    whole = pl.BlockSpec(memory_space=pltpu.VMEM)
    return pl.pallas_call(
        pack_kernel,
        in_specs=[pl.BlockSpec(memory_space=pltpu.SMEM)] + [pl.BlockSpec(memory_space=pl.ANY)] * 6,
        out_specs=(whole,) * 8,
        out_shape=tuple(jax.ShapeDtypeStruct((IN_ROWS + (0 if d % 2 else SLAB), 128), BF) for d in range(8)),
        scratch_shapes=[
            *[pltpu.VMEM((128, 1536), BF)] * 4,
            pltpu.VMEM((12, 128), BF),
            pltpu.VMEM((128, 3072), BF),
            pltpu.SemaphoreType.DMA((6,)),
        ],
        compiler_params=pltpu.CompilerParams(vmem_limit_bytes=WHOLE_GRANT),
        name="pack",
    )(me, q, k, v, o, norms, out_grad)


def product(shard_ref, g, yh):
    return dot(shard_ref[yh, 0], g[:, :384], NT_DIMS) + dot(shard_ref[yh, 1], g[:, 384:], NT_DIMS)


def project_own_kernel(where_ref, own_ref, g0_ref, g1_ref, g2_ref, g3_ref, part_ref, g_ref):
    for e, ref in enumerate((g0_ref, g1_ref, g2_ref, g3_ref)):
        rows = pl.ds(pl.multiple_of(128 * jnp.bitwise_xor(where_ref[1], e), 128), 128)
        for n in range(6):
            g_ref[rows, 128 * n : 128 * (n + 1)] = ref[128 * n : 128 * (n + 1)]
    for yh in range(2):
        part_ref[yh] = product(own_ref, g_ref[...], yh)


def project_own(where, own, slabs):
    whole = pl.BlockSpec(memory_space=pltpu.VMEM)
    slab = pl.BlockSpec((SLAB, 128), lambda i: (0, 0))
    return pl.pallas_call(
        project_own_kernel,
        grid=(1,),
        in_specs=[pl.BlockSpec(memory_space=pltpu.SMEM), whole] + [slab] * 4,
        out_specs=(whole, whole),
        out_shape=(jax.ShapeDtypeStruct((2, 384, 512), F32), jax.ShapeDtypeStruct((512, 768), BF)),
        compiler_params=pltpu.CompilerParams(vmem_limit_bytes=GRANT),
        name="project_own",
    )(where, own, *slabs)


def project_kernel(where_ref, part_ref, other_ref, g_ref, out_ref, t_ref):
    core = where_ref[0]
    for yh in range(2):
        for c, part in ((core, part_ref[yh]), (1 - core, product(other_ref, g_ref[...], yh))):
            for z in range(16):
                rows = pl.ds(pl.multiple_of(24 * c + (96 * z + 48 * yh), 8), 24)
                t_ref[rows] = part[24 * z : 24 * (z + 1)]
    for x in range(4):
        for j in range(2):
            head = 3 * x + j
            block = t_ref[128 * head : 128 * (head + 1)].astype(BF)
            for n in range(4):
                out_ref[2 * x + j, 128 * n : 128 * (n + 1)] = block[:, 128 * n : 128 * (n + 1)]
        head = 3 * x + 2
        block = t_ref[128 * head : 128 * (head + 1)].astype(BF)
        for j in range(2):
            for e in range(2):
                at = 256 * e + 64 * j
                out_ref[2 * x + j, 512 + 128 * e : 640 + 128 * e] = jnp.concatenate(
                    [block[:, at : at + 64], block[:, at + 128 : at + 192]], axis=1
                )


def project(where, part, other, g):
    whole = pl.BlockSpec(memory_space=pltpu.VMEM)
    return pl.pallas_call(
        project_kernel,
        in_specs=[pl.BlockSpec(memory_space=pltpu.SMEM), whole, whole, whole],
        out_specs=whole,
        out_shape=jax.ShapeDtypeStruct((8, 768, 128), BF),
        scratch_shapes=[pltpu.VMEM((1536, 512), F32)],
        compiler_params=pltpu.CompilerParams(vmem_limit_bytes=GRANT),
        name="project",
    )(where, part, other, g)


def attend_unit(in_ref, g_ref, mask_ref, out_ref, dk_ref, dv_ref, per, rows, norm_row, outs):
    q0, o0, k0, v0, g0 = rows
    gq0, gk0, gv0 = outs
    group = 256 // per
    keys = 1024
    chunk = 256
    for b in range(8 // group):
        sources = range(group * b, group * (b + 1))
        q = jnp.concatenate([in_ref[s, q0 : q0 + per] for s in sources], axis=0)
        o = jnp.concatenate([in_ref[s, o0 : o0 + per] for s in sources], axis=0)
        g = g_ref[g0 + 256 * b : g0 + 256 * (b + 1)]
        product = g.astype(F32) * o.astype(F32)
        dots = lax.dot_general(
            jnp.ones((8, 128), F32), product, NT_DIMS, precision=lax.Precision.HIGHEST, preferred_element_type=F32
        )[0:1]
        dots = dots.astype(BF).astype(F32)
        norm = norm_row(b)
        dq = jnp.zeros((HD, 256), F32)
        for n in range(keys // chunk):
            src = slice(2 * n, 2 * n + 2)
            k = in_ref[src, k0 : k0 + 128].reshape(chunk, HD)
            v = in_ref[src, v0 : v0 + 128].reshape(chunk, HD)
            scores = dot(k, q, NT_DIMS)
            prob = jnp.exp2(scores * (SCALE * LOG2E) - norm)
            allowed = mask_ref[4 * n : 4 * (n + 1), 256 * b : 256 * (b + 1)]
            prob = (prob.reshape(4, TILE, 256) * allowed[:, None, :]).reshape(chunk, 256)
            score_grad = prob * (dot(v, g, NT_DIMS) - dots)
            prob = prob.astype(BF)
            score_grad = score_grad.astype(BF)
            dv = dot(prob, g, NN_DIMS)
            dk = dot(score_grad, q, NN_DIMS)
            at = slice(chunk * n, chunk * (n + 1))
            if b == 0:
                dv_ref[at] = dv
                dk_ref[at] = dk
            else:
                dv_ref[at] += dv
                dk_ref[at] += dk
            dq = dq + dot(k, score_grad, TN_DIMS)
        dq = (dq.T * SCALE).astype(BF)
        for e, s in enumerate(sources):
            out_ref[s, gq0 : gq0 + per] = dq[per * e : per * (e + 1)]
    for s in range(8):
        at = slice(128 * s, 128 * (s + 1))
        out_ref[s, gk0 : gk0 + 128] = (dk_ref[at] * SCALE).astype(BF)
        out_ref[s, gv0 : gv0 + 128] = dv_ref[at].astype(BF)


def attend_kernel(me_ref, *refs):
    sent_refs = refs[:8]
    mid_ref, mask_a_hbm, mask_c_hbm, out_ref, in_ref, g_ref, dk_ref, dv_ref, mask_a_ref, mask_c_ref, sems = refs[8:]
    sources = [ref if d % 2 else ref.at[pl.ds(SLAB, IN_ROWS)] for d, ref in enumerate(sent_refs)]
    targets = [in_ref.at[jnp.bitwise_xor(me_ref[0], d)] for d in range(8)]
    copies = start((*sources, mask_a_hbm, mask_c_hbm), (*targets, mask_a_ref, mask_c_ref), sems)
    for y in range(2):
        for n in range(6):
            total = mid_ref[y, 128 * n : 128 * (n + 1)].astype(F32)
            for x in range(1, 4):
                total = total + mid_ref[2 * x + y, 128 * n : 128 * (n + 1)].astype(F32)
            total = total.astype(BF).T
            if n < 4:
                at = 128 * (2 * n + y)
                g_ref[at : at + 128] = total
            else:
                for e in range(2):
                    at = 1024 + 64 * (4 * (n - 4) + 2 * e + y)
                    g_ref[at : at + 64] = total[64 * e : 64 * (e + 1)]
    for copy in copies:
        copy.wait()
    second = me_ref[0] % 2 == 1

    def norm_a(b):
        parts = [in_ref[s, NR : NR + 16].astype(F32)[0:1] for s in (2 * b, 2 * b + 1)]
        return jnp.concatenate(parts, axis=1) * LOG2E

    def norm_c(b):
        parts = []
        for s in range(4 * b, 4 * b + 4):
            row = in_ref[s, NR : NR + 16].astype(F32)[1:2]
            parts.append(jnp.where(second, row[:, 64:], row[:, :64]))
        return jnp.concatenate(parts, axis=1) * LOG2E

    attend_unit(
        in_ref, g_ref, mask_a_ref, out_ref, dk_ref, dv_ref, 128, (QA, OA, KA, VA, 0), norm_a, (GQA, GKA, GVA)
    )
    attend_unit(
        in_ref, g_ref, mask_c_ref, out_ref, dk_ref, dv_ref, 64, (QC, OC, KC, VC, 1024), norm_c, (GQC, GKC, GVC)
    )


def attend(me, arrived, partial, mask_a, mask_c):
    whole = pl.BlockSpec(memory_space=pltpu.VMEM)
    return pl.pallas_call(
        attend_kernel,
        in_specs=[pl.BlockSpec(memory_space=pltpu.SMEM)]
        + [pl.BlockSpec(memory_space=pl.ANY)] * 8
        + [whole]
        + [pl.BlockSpec(memory_space=pl.ANY)] * 2,
        out_specs=whole,
        out_shape=jax.ShapeDtypeStruct((8, OUT_ROWS, 128), BF),
        scratch_shapes=[
            pltpu.VMEM((8, IN_ROWS, 128), BF),
            pltpu.VMEM((1536, 128), BF),
            pltpu.VMEM((1024, 128), F32),
            pltpu.VMEM((1024, 128), F32),
            pltpu.VMEM((16, 1024), F32),
            pltpu.VMEM((16, 512), F32),
            pltpu.SemaphoreType.DMA((10,)),
        ],
        compiler_params=pltpu.CompilerParams(vmem_limit_bytes=GRANT),
        name="attend",
    )(me, *arrived, partial, mask_a, mask_c)


def merge_kernel(in_ref, gq_ref, gk_ref, gv_ref):
    for j in range(2):
        own = slice(HD * j, HD * (j + 1))
        gq_ref[0, :, own] = in_ref[j, GQA : GQA + 128]
        gk_ref[0, :, own] = in_ref[j, GKA : GKA + 128]
        gv_ref[0, :, own] = in_ref[j, GVA : GVA + 128]
        gq_ref[0, TILE * j : TILE * (j + 1), 2 * HD :] = in_ref[j, GQC : GQC + 64]
    for ref, at in ((gk_ref, GKC), (gv_ref, GVC)):
        total = in_ref[0, at : at + 128].astype(F32) + in_ref[1, at : at + 128].astype(F32)
        ref[0, :, 2 * HD :] = total.astype(BF)


def merge(arrived):
    out = pl.BlockSpec((1, 128, 3 * HD), lambda i: (0, 0, i))
    shape = jax.ShapeDtypeStruct((1, 128, 1536), BF)
    return pl.pallas_call(
        merge_kernel,
        grid=(4,),
        in_specs=[pl.BlockSpec((2, OUT_ROWS, 128), lambda i: (i, 0, 0))],
        out_specs=(out, out, out),
        out_shape=(shape, shape, shape),
        compiler_params=pltpu.CompilerParams(vmem_limit_bytes=GRANT),
        name="merge",
    )(arrived)


def exchange(array, axes):
    return lax.all_to_all(array, axes, split_axis=0, concat_axis=0, tiled=True)


def spread(array, axes, count):
    return exchange(jnp.broadcast_to(array[None], (count,) + array.shape), axes)


def gather_weight(proj_weight):
    own = spread(proj_weight, "z", 16)
    own = spread(own, ("yh", "yl"), 4).reshape(2, 2, 384, 384)
    other = lax.ppermute(own, "core", [(0, 1), (1, 0)])
    return own, other


def mask_kernel(shared, where_ref, table_ref, out_ref):
    x, y = where_ref[0] // 2, where_ref[0] % 2
    tile = lax.broadcasted_iota(jnp.int32, out_ref.shape, 0)
    group = lax.broadcasted_iota(jnp.int32, out_ref.shape, 1) // TILE
    of_lane = 2 * group + y if shared else group
    head = 3 * x + 2 if shared else 3 * x + y
    out_ref[...] = dot(table_ref[0, head].astype(F32), jnp.where(tile == of_lane, 1.0, 0.0), TN_DIMS)


def mask_rows(me, tile_mask, shared):
    whole = pl.BlockSpec(memory_space=pltpu.VMEM)
    return pl.pallas_call(
        functools.partial(mask_kernel, shared),
        in_specs=[pl.BlockSpec(memory_space=pltpu.SMEM), whole],
        out_specs=whole,
        out_shape=jax.ShapeDtypeStruct((16, 512 if shared else 1024), F32),
        compiler_params=pltpu.CompilerParams(vmem_limit_bytes=GRANT),
        name="mask",
    )(me, tile_mask)


def swap(array, d):
    return lax.ppermute(array, ("x", "yl"), [(s, s ^ d) for s in range(8)])


def after_weight(q, k, v, o, log_norm, out_grad, own, other, core, tile_mask):
    x, y = lax.axis_index("x"), lax.axis_index("yl")
    me = (2 * x + y).reshape(1)
    where = jnp.stack([core, x])
    sent = pack(me, q[0], k[0], v[0], o[0], log_norm[0].T, out_grad[0])
    arrived = [sent[d] if d in (0, 4, 5) else swap(sent[d], d) for d in range(8)]
    arrived[4] = swap(swap(sent[4], 6), 2)
    arrived[5] = swap(swap(sent[5], 3), 6)
    part, slab = project_own(where, own, arrived[::2])
    partial = exchange(project(where, part, other, slab), ("x", "yl"))
    mask_a, mask_c = mask_rows(me, tile_mask, False), mask_rows(me, tile_mask, True)
    result = exchange(attend(me, arrived, partial, mask_a, mask_c), ("x", "yl"))
    return merge(result)


def local(queries, key_states, value_states, attn_out, log_norm, out_grad, proj_weight, tile_mask):
    own, other = gather_weight(proj_weight)
    return after_weight(
        queries,
        key_states,
        value_states,
        attn_out,
        log_norm,
        out_grad,
        own,
        other,
        lax.axis_index("core"),
        tile_mask,
    )


def solution(mesh):
    inner = Mesh(mesh.devices.reshape(16, 2, 2, 4, 2), ("z", "yh", "core", "x", "yl"))
    clips, tokens = ("z", "yh", "core"), ("x", "yl")
    rows = P(clips, tokens, None)
    return jax.shard_map(
        local,
        mesh=inner,
        in_specs=(rows,) * 6 + (P(clips, tokens), P(clips, None, None, None)),
        out_specs=(rows, rows, rows),
        check_vma=False,
    )
```

```python
import functools
import math

import jax
import jax.numpy as jnp
from jax import lax
from jax.experimental import pallas as pl
from jax.experimental.pallas import tpu as pltpu
from jax.sharding import Mesh, PartitionSpec as P


BF = jnp.bfloat16
F32 = jnp.float32
HD = 128
TILE = 64
SCALE = HD**-0.5
LOG2E = math.log2(math.e)

QA, KA, VA, OA, KC, VC, QC, OC, NR = 0, 128, 256, 384, 512, 640, 768, 832, 896
IN_ROWS = 912
SLAB = 768
GRANT = 16 << 20
WHOLE_GRANT = 62 << 20
GQA, GKA, GVA, GKC, GVC, GQC = 0, 128, 256, 384, 512, 640
OUT_ROWS = 704

NT_DIMS = (((1,), (1,)), ((), ()))
NN_DIMS = (((1,), (0,)), ((), ()))
TN_DIMS = (((0,), (0,)), ((), ()))


def dot(a, b, dims):
    return lax.dot_general(a, b, dims, preferred_element_type=F32)


def start(sources, targets, sems):
    copies = [pltpu.make_async_copy(a, b, sems.at[n]) for n, (a, b) in enumerate(zip(sources, targets, strict=True))]
    for copy in copies:
        copy.start()
    return copies


def pack_kernel(me_ref, q_hbm, k_hbm, v_hbm, o_hbm, n_hbm, g_hbm, *refs):
    out_refs = refs[:8]
    q_ref, k_ref, v_ref, o_ref, n_ref, g_ref, sems = refs[8:]
    for copy in start((q_hbm, k_hbm, v_hbm, o_hbm, n_hbm, g_hbm), (q_ref, k_ref, v_ref, o_ref, n_ref, g_ref), sems):
        copy.wait()
    for d, out_ref in enumerate(out_refs):
        to = jnp.bitwise_xor(me_ref[0], d)
        x, y = to // 2, to % 2
        base = 0 if d % 2 else SLAB
        own = pl.ds(pl.multiple_of(HD * (3 * x + y), HD), HD)
        shared = pl.ds(pl.multiple_of(HD * (3 * x + 2), HD), HD)
        half = pl.ds(pl.multiple_of(TILE * y, TILE), TILE)
        if base:
            for e in range(6):
                columns = pl.ds(pl.multiple_of(768 * x + 128 * e, 128), 128)
                out_ref[128 * e : 128 * (e + 1)] = g_ref[:, columns]
        for ref, at in ((q_ref, QA), (k_ref, KA), (v_ref, VA), (o_ref, OA)):
            out_ref[base + at : base + at + 128] = ref[:, own]
        for ref, at in ((k_ref, KC), (v_ref, VC)):
            out_ref[base + at : base + at + 128] = ref[:, shared]
        for ref, at in ((q_ref, QC), (o_ref, OC)):
            out_ref[base + at : base + at + 64] = ref[half, shared]
        line = lax.broadcasted_iota(jnp.int32, (16, 12), 0)
        head = lax.broadcasted_iota(jnp.int32, (16, 12), 1)
        wanted = jnp.where(line == 0, 3 * x + y, 3 * x + 2)
        pick = jnp.where((head == wanted) & (line < 2), 1.0, 0.0).astype(BF)
        out_ref[base + NR : base + IN_ROWS] = dot(pick, n_ref[...], NN_DIMS).astype(BF)


def pack(me, q, k, v, o, norms, out_grad):
    whole = pl.BlockSpec(memory_space=pltpu.VMEM)
    return pl.pallas_call(
        pack_kernel,
        in_specs=[pl.BlockSpec(memory_space=pltpu.SMEM)] + [pl.BlockSpec(memory_space=pl.ANY)] * 6,
        out_specs=(whole,) * 8,
        out_shape=tuple(jax.ShapeDtypeStruct((IN_ROWS + (0 if d % 2 else SLAB), 128), BF) for d in range(8)),
        scratch_shapes=[
            *[pltpu.VMEM((128, 1536), BF)] * 4,
            pltpu.VMEM((12, 128), BF),
            pltpu.VMEM((128, 3072), BF),
            pltpu.SemaphoreType.DMA((6,)),
        ],
        compiler_params=pltpu.CompilerParams(vmem_limit_bytes=WHOLE_GRANT),
        name="pack",
    )(me, q, k, v, o, norms, out_grad)


def product(shard_ref, g, yh):
    return dot(shard_ref[yh, 0], g[:, :384], NT_DIMS) + dot(shard_ref[yh, 1], g[:, 384:], NT_DIMS)


def project_own_kernel(where_ref, own_ref, g0_ref, g1_ref, g2_ref, g3_ref, part_ref, g_ref):
    for e, ref in enumerate((g0_ref, g1_ref, g2_ref, g3_ref)):
        rows = pl.ds(pl.multiple_of(128 * jnp.bitwise_xor(where_ref[1], e), 128), 128)
        for n in range(6):
            g_ref[rows, 128 * n : 128 * (n + 1)] = ref[128 * n : 128 * (n + 1)]
    for yh in range(2):
        part_ref[yh] = product(own_ref, g_ref[...], yh)


def project_own(where, own, slabs):
    whole = pl.BlockSpec(memory_space=pltpu.VMEM)
    slab = pl.BlockSpec((SLAB, 128), lambda i: (0, 0))
    return pl.pallas_call(
        project_own_kernel,
        grid=(1,),
        in_specs=[pl.BlockSpec(memory_space=pltpu.SMEM), whole] + [slab] * 4,
        out_specs=(whole, whole),
        out_shape=(jax.ShapeDtypeStruct((2, 384, 512), F32), jax.ShapeDtypeStruct((512, 768), BF)),
        compiler_params=pltpu.CompilerParams(vmem_limit_bytes=GRANT),
        name="project_own",
    )(where, own, *slabs)


def project_kernel(where_ref, part_ref, other_ref, g_ref, out_ref, t_ref):
    core = where_ref[0]
    for yh in range(2):
        for c, part in ((core, part_ref[yh]), (1 - core, product(other_ref, g_ref[...], yh))):
            for z in range(16):
                rows = pl.ds(pl.multiple_of(24 * c + (96 * z + 48 * yh), 8), 24)
                t_ref[rows] = part[24 * z : 24 * (z + 1)]
    for x in range(4):
        for j in range(2):
            head = 3 * x + j
            block = t_ref[128 * head : 128 * (head + 1)].astype(BF)
            for n in range(4):
                out_ref[2 * x + j, 128 * n : 128 * (n + 1)] = block[:, 128 * n : 128 * (n + 1)]
        head = 3 * x + 2
        block = t_ref[128 * head : 128 * (head + 1)].astype(BF)
        for j in range(2):
            for e in range(2):
                at = 256 * e + 64 * j
                out_ref[2 * x + j, 512 + 128 * e : 640 + 128 * e] = jnp.concatenate(
                    [block[:, at : at + 64], block[:, at + 128 : at + 192]], axis=1
                )


def project(where, part, other, g):
    whole = pl.BlockSpec(memory_space=pltpu.VMEM)
    return pl.pallas_call(
        project_kernel,
        in_specs=[pl.BlockSpec(memory_space=pltpu.SMEM), whole, whole, whole],
        out_specs=whole,
        out_shape=jax.ShapeDtypeStruct((8, 768, 128), BF),
        scratch_shapes=[pltpu.VMEM((1536, 512), F32)],
        compiler_params=pltpu.CompilerParams(vmem_limit_bytes=GRANT),
        name="project",
    )(where, part, other, g)


def attend_unit(in_ref, g_ref, mask_ref, out_ref, dk_ref, dv_ref, per, rows, norm_row, outs):
    q0, o0, k0, v0, g0 = rows
    gq0, gk0, gv0 = outs
    group = 256 // per
    keys = 1024
    chunk = 1024
    for b in range(8 // group):
        sources = range(group * b, group * (b + 1))
        q = jnp.concatenate([in_ref[s, q0 : q0 + per] for s in sources], axis=0)
        o = jnp.concatenate([in_ref[s, o0 : o0 + per] for s in sources], axis=0)
        g = g_ref[g0 + 256 * b : g0 + 256 * (b + 1)]
        product = g.astype(F32) * o.astype(F32)
        dots = lax.dot_general(
            jnp.ones((8, 128), F32), product, NT_DIMS, precision=lax.Precision.HIGHEST, preferred_element_type=F32
        )[0:1]
        dots = dots.astype(BF).astype(F32)
        norm = norm_row(b)
        dq = jnp.zeros((HD, 256), F32)
        for n in range(keys // chunk):
            src = slice(chunk // 128 * n, chunk // 128 * (n + 1))
            k = in_ref[src, k0 : k0 + 128].reshape(chunk, HD)
            v = in_ref[src, v0 : v0 + 128].reshape(chunk, HD)
            scores = dot(k, q, NT_DIMS)
            prob = jnp.exp2(scores * (SCALE * LOG2E) - norm)
            allowed = mask_ref[chunk // TILE * n : chunk // TILE * (n + 1), 256 * b : 256 * (b + 1)]
            prob = (prob.reshape(chunk // TILE, TILE, 256) * allowed[:, None, :]).reshape(chunk, 256)
            score_grad = prob * (dot(v, g, NT_DIMS) - dots)
            prob = prob.astype(BF)
            score_grad = score_grad.astype(BF)
            dv = dot(prob, g, NN_DIMS)
            dk = dot(score_grad, q, NN_DIMS)
            at = slice(chunk * n, chunk * (n + 1))
            if b == 0:
                dv_ref[at] = dv
                dk_ref[at] = dk
            else:
                dv_ref[at] += dv
                dk_ref[at] += dk
            dq = dq + dot(k, score_grad, TN_DIMS)
        dq = (dq.T * SCALE).astype(BF)
        for e, s in enumerate(sources):
            out_ref[s, gq0 : gq0 + per] = dq[per * e : per * (e + 1)]
    for s in range(8):
        at = slice(128 * s, 128 * (s + 1))
        out_ref[s, gk0 : gk0 + 128] = (dk_ref[at] * SCALE).astype(BF)
        out_ref[s, gv0 : gv0 + 128] = dv_ref[at].astype(BF)


def attend_kernel(me_ref, *refs):
    sent_refs = refs[:8]
    mid_ref, mask_a_hbm, mask_c_hbm, out_ref, in_ref, g_ref, dk_ref, dv_ref, mask_a_ref, mask_c_ref, sems = refs[8:]
    sources = [ref if d % 2 else ref.at[pl.ds(SLAB, IN_ROWS)] for d, ref in enumerate(sent_refs)]
    targets = [in_ref.at[jnp.bitwise_xor(me_ref[0], d)] for d in range(8)]
    copies = start((*sources, mask_a_hbm, mask_c_hbm), (*targets, mask_a_ref, mask_c_ref), sems)
    for y in range(2):
        for n in range(6):
            total = mid_ref[y, 128 * n : 128 * (n + 1)].astype(F32)
            for x in range(1, 4):
                total = total + mid_ref[2 * x + y, 128 * n : 128 * (n + 1)].astype(F32)
            total = total.astype(BF).T
            if n < 4:
                at = 128 * (2 * n + y)
                g_ref[at : at + 128] = total
            else:
                for e in range(2):
                    at = 1024 + 64 * (4 * (n - 4) + 2 * e + y)
                    g_ref[at : at + 64] = total[64 * e : 64 * (e + 1)]
    for copy in copies:
        copy.wait()
    second = me_ref[0] % 2 == 1

    def norm_a(b):
        parts = [in_ref[s, NR : NR + 16].astype(F32)[0:1] for s in (2 * b, 2 * b + 1)]
        return jnp.concatenate(parts, axis=1) * LOG2E

    def norm_c(b):
        parts = []
        for s in range(4 * b, 4 * b + 4):
            row = in_ref[s, NR : NR + 16].astype(F32)[1:2]
            parts.append(jnp.where(second, row[:, 64:], row[:, :64]))
        return jnp.concatenate(parts, axis=1) * LOG2E

    attend_unit(
        in_ref, g_ref, mask_a_ref, out_ref, dk_ref, dv_ref, 128, (QA, OA, KA, VA, 0), norm_a, (GQA, GKA, GVA)
    )
    attend_unit(
        in_ref, g_ref, mask_c_ref, out_ref, dk_ref, dv_ref, 64, (QC, OC, KC, VC, 1024), norm_c, (GQC, GKC, GVC)
    )


def attend(me, arrived, partial, mask_a, mask_c):
    whole = pl.BlockSpec(memory_space=pltpu.VMEM)
    return pl.pallas_call(
        attend_kernel,
        in_specs=[pl.BlockSpec(memory_space=pltpu.SMEM)]
        + [pl.BlockSpec(memory_space=pl.ANY)] * 8
        + [whole]
        + [pl.BlockSpec(memory_space=pl.ANY)] * 2,
        out_specs=whole,
        out_shape=jax.ShapeDtypeStruct((8, OUT_ROWS, 128), BF),
        scratch_shapes=[
            pltpu.VMEM((8, IN_ROWS, 128), BF),
            pltpu.VMEM((1536, 128), BF),
            pltpu.VMEM((1024, 128), F32),
            pltpu.VMEM((1024, 128), F32),
            pltpu.VMEM((16, 1024), F32),
            pltpu.VMEM((16, 512), F32),
            pltpu.SemaphoreType.DMA((10,)),
        ],
        compiler_params=pltpu.CompilerParams(vmem_limit_bytes=GRANT),
        name="attend",
    )(me, *arrived, partial, mask_a, mask_c)


def merge_kernel(in_ref, gq_ref, gk_ref, gv_ref):
    for j in range(2):
        own = slice(HD * j, HD * (j + 1))
        gq_ref[0, :, own] = in_ref[j, GQA : GQA + 128]
        gk_ref[0, :, own] = in_ref[j, GKA : GKA + 128]
        gv_ref[0, :, own] = in_ref[j, GVA : GVA + 128]
        gq_ref[0, TILE * j : TILE * (j + 1), 2 * HD :] = in_ref[j, GQC : GQC + 64]
    for ref, at in ((gk_ref, GKC), (gv_ref, GVC)):
        total = in_ref[0, at : at + 128].astype(F32) + in_ref[1, at : at + 128].astype(F32)
        ref[0, :, 2 * HD :] = total.astype(BF)


def merge(arrived):
    out = pl.BlockSpec((1, 128, 3 * HD), lambda i: (0, 0, i))
    shape = jax.ShapeDtypeStruct((1, 128, 1536), BF)
    return pl.pallas_call(
        merge_kernel,
        grid=(4,),
        in_specs=[pl.BlockSpec((2, OUT_ROWS, 128), lambda i: (i, 0, 0))],
        out_specs=(out, out, out),
        out_shape=(shape, shape, shape),
        compiler_params=pltpu.CompilerParams(vmem_limit_bytes=GRANT),
        name="merge",
    )(arrived)


def exchange(array, axes):
    return lax.all_to_all(array, axes, split_axis=0, concat_axis=0, tiled=True)


def spread(array, axes, count):
    return exchange(jnp.broadcast_to(array[None], (count,) + array.shape), axes)


def gather_weight(proj_weight):
    own = spread(proj_weight, "z", 16)
    own = spread(own, ("yh", "yl"), 4).reshape(2, 2, 384, 384)
    other = lax.ppermute(own, "core", [(0, 1), (1, 0)])
    return own, other


def mask_kernel(shared, where_ref, table_ref, out_ref):
    x, y = where_ref[0] // 2, where_ref[0] % 2
    tile = lax.broadcasted_iota(jnp.int32, out_ref.shape, 0)
    group = lax.broadcasted_iota(jnp.int32, out_ref.shape, 1) // TILE
    of_lane = 2 * group + y if shared else group
    head = 3 * x + 2 if shared else 3 * x + y
    out_ref[...] = dot(table_ref[0, head].astype(F32), jnp.where(tile == of_lane, 1.0, 0.0), TN_DIMS)


def mask_rows(me, tile_mask, shared):
    whole = pl.BlockSpec(memory_space=pltpu.VMEM)
    return pl.pallas_call(
        functools.partial(mask_kernel, shared),
        in_specs=[pl.BlockSpec(memory_space=pltpu.SMEM), whole],
        out_specs=whole,
        out_shape=jax.ShapeDtypeStruct((16, 512 if shared else 1024), F32),
        compiler_params=pltpu.CompilerParams(vmem_limit_bytes=GRANT),
        name="mask",
    )(me, tile_mask)


def swap(array, d):
    return lax.ppermute(array, ("x", "yl"), [(s, s ^ d) for s in range(8)])


def after_weight(q, k, v, o, log_norm, out_grad, own, other, core, tile_mask):
    x, y = lax.axis_index("x"), lax.axis_index("yl")
    me = (2 * x + y).reshape(1)
    where = jnp.stack([core, x])
    sent = pack(me, q[0], k[0], v[0], o[0], log_norm[0].T, out_grad[0])
    arrived = [sent[d] if d in (0, 4, 5) else swap(sent[d], d) for d in range(8)]
    arrived[4] = swap(swap(sent[4], 6), 2)
    arrived[5] = swap(swap(sent[5], 3), 6)
    part, slab = project_own(where, own, arrived[::2])
    part = project(where, part, other, slab)
    partial = exchange(part, ("x", "yl"))
    mask_a, mask_c = mask_rows(me, tile_mask, False), mask_rows(me, tile_mask, True)
    result = exchange(attend(me, arrived, partial, mask_a, mask_c), ("x", "yl"))
    return merge(result)


def local(queries, key_states, value_states, attn_out, log_norm, out_grad, proj_weight, tile_mask):
    own, other = gather_weight(proj_weight)
    return after_weight(
        queries,
        key_states,
        value_states,
        attn_out,
        log_norm,
        out_grad,
        own,
        other,
        lax.axis_index("core"),
        tile_mask,
    )


def solution(mesh):
    inner = Mesh(mesh.devices.reshape(16, 2, 2, 4, 2), ("z", "yh", "core", "x", "yl"))
    clips, tokens = ("z", "yh", "core"), ("x", "yl")
    rows = P(clips, tokens, None)
    return jax.shard_map(
        local,
        mesh=inner,
        in_specs=(rows,) * 6 + (P(clips, tokens), P(clips, None, None, None)),
        out_specs=(rows, rows, rows),
        check_vma=False,
    )
```

```python
import functools
import math

import jax
import jax.numpy as jnp
from jax import lax
from jax.experimental import pallas as pl
from jax.experimental.pallas import tpu as pltpu
from jax.sharding import Mesh, PartitionSpec as P


BF = jnp.bfloat16
F32 = jnp.float32
HD = 128
TILE = 64
SCALE = HD**-0.5
LOG2E = math.log2(math.e)

QA, KA, VA, OA, KC, VC, QC, OC, NR = 0, 128, 256, 384, 512, 640, 768, 832, 896
IN_ROWS = 912
SLAB = 768
GRANT = 16 << 20
WHOLE_GRANT = 62 << 20
GQA, GKA, GVA, GKC, GVC, GQC = 0, 128, 256, 384, 512, 640
OUT_ROWS = 704

PARTNERS = ((0, 0), (1, 3), (2, 6), (3, 7), (6, 2), (7, 1), (4, 4), (5, 5))

NT_DIMS = (((1,), (1,)), ((), ()))
NN_DIMS = (((1,), (0,)), ((), ()))
TN_DIMS = (((0,), (0,)), ((), ()))


def dot(a, b, dims):
    return lax.dot_general(a, b, dims, preferred_element_type=F32)


def partner(me_ref, slot):
    first, second = PARTNERS[slot]
    return jnp.bitwise_xor(me_ref[0], jnp.where(me_ref[1] == 0, first, second))


def start(sources, targets, sems):
    copies = [pltpu.make_async_copy(a, b, sems.at[n]) for n, (a, b) in enumerate(zip(sources, targets, strict=True))]
    for copy in copies:
        copy.start()
    return copies


def pack_kernel(me_ref, q_hbm, k_hbm, v_hbm, o_hbm, n_hbm, g_hbm, *refs):
    out_refs = refs[:8]
    q_ref, k_ref, v_ref, o_ref, n_ref, g_ref, sems = refs[8:]
    for copy in start((q_hbm, k_hbm, v_hbm, o_hbm, n_hbm, g_hbm), (q_ref, k_ref, v_ref, o_ref, n_ref, g_ref), sems):
        copy.wait()
    for d, out_ref in enumerate(out_refs):
        to = partner(me_ref, d)
        x, y = to // 2, to % 2
        base = 0 if d % 2 else SLAB
        own = pl.ds(pl.multiple_of(HD * (3 * x + y), HD), HD)
        shared = pl.ds(pl.multiple_of(HD * (3 * x + 2), HD), HD)
        half = pl.ds(pl.multiple_of(TILE * y, TILE), TILE)
        if base:
            for e in range(6):
                columns = pl.ds(pl.multiple_of(768 * x + 128 * e, 128), 128)
                out_ref[128 * e : 128 * (e + 1)] = g_ref[:, columns]
        for ref, at in ((q_ref, QA), (k_ref, KA), (v_ref, VA), (o_ref, OA)):
            out_ref[base + at : base + at + 128] = ref[:, own]
        for ref, at in ((k_ref, KC), (v_ref, VC)):
            out_ref[base + at : base + at + 128] = ref[:, shared]
        for ref, at in ((q_ref, QC), (o_ref, OC)):
            out_ref[base + at : base + at + 64] = ref[half, shared]
        line = lax.broadcasted_iota(jnp.int32, (16, 12), 0)
        head = lax.broadcasted_iota(jnp.int32, (16, 12), 1)
        wanted = jnp.where(line == 0, 3 * x + y, 3 * x + 2)
        pick = jnp.where((head == wanted) & (line < 2), 1.0, 0.0).astype(BF)
        out_ref[base + NR : base + IN_ROWS] = dot(pick, n_ref[...], NN_DIMS).astype(BF)


def pack(me, q, k, v, o, norms, out_grad):
    whole = pl.BlockSpec(memory_space=pltpu.VMEM)
    return pl.pallas_call(
        pack_kernel,
        in_specs=[pl.BlockSpec(memory_space=pltpu.SMEM)] + [pl.BlockSpec(memory_space=pl.ANY)] * 6,
        out_specs=(whole,) * 8,
        out_shape=tuple(jax.ShapeDtypeStruct((IN_ROWS + (0 if d % 2 else SLAB), 128), BF) for d in range(8)),
        scratch_shapes=[
            *[pltpu.VMEM((128, 1536), BF)] * 4,
            pltpu.VMEM((12, 128), BF),
            pltpu.VMEM((128, 3072), BF),
            pltpu.SemaphoreType.DMA((6,)),
        ],
        compiler_params=pltpu.CompilerParams(vmem_limit_bytes=WHOLE_GRANT),
        name="pack",
    )(me, q, k, v, o, norms, out_grad)


def product(shard_ref, g, yh):
    return dot(shard_ref[yh, 0], g[:, :384], NT_DIMS) + dot(shard_ref[yh, 1], g[:, 384:], NT_DIMS)


def project_own_kernel(me_ref, own_ref, g0_ref, g1_ref, g2_ref, g3_ref, part_ref, g_ref):
    for e, ref in enumerate((g0_ref, g1_ref, g2_ref, g3_ref)):
        rows = pl.ds(pl.multiple_of(128 * (partner(me_ref, 2 * e) // 2), 128), 128)
        for n in range(6):
            g_ref[rows, 128 * n : 128 * (n + 1)] = ref[128 * n : 128 * (n + 1)]
    for yh in range(2):
        part_ref[yh] = product(own_ref, g_ref[...], yh)


def project_own(me, own, slabs):
    whole = pl.BlockSpec(memory_space=pltpu.VMEM)
    slab = pl.BlockSpec((SLAB, 128), lambda i: (0, 0))
    return pl.pallas_call(
        project_own_kernel,
        grid=(1,),
        in_specs=[pl.BlockSpec(memory_space=pltpu.SMEM), whole] + [slab] * 4,
        out_specs=(whole, whole),
        out_shape=(jax.ShapeDtypeStruct((2, 384, 512), F32), jax.ShapeDtypeStruct((512, 768), BF)),
        compiler_params=pltpu.CompilerParams(vmem_limit_bytes=GRANT),
        name="project_own",
    )(me, own, *slabs)


def project_kernel(me_ref, part_ref, other_ref, g_ref, out_ref, t_ref):
    core = me_ref[1]
    for yh in range(2):
        for c, part in ((core, part_ref[yh]), (1 - core, product(other_ref, g_ref[...], yh))):
            for z in range(16):
                rows = pl.ds(pl.multiple_of(24 * c + (96 * z + 48 * yh), 8), 24)
                t_ref[rows] = part[24 * z : 24 * (z + 1)]
    for x in range(4):
        for j in range(2):
            head = 3 * x + j
            block = t_ref[128 * head : 128 * (head + 1)].astype(BF)
            for n in range(4):
                out_ref[2 * x + j, 128 * n : 128 * (n + 1)] = block[:, 128 * n : 128 * (n + 1)]
        head = 3 * x + 2
        block = t_ref[128 * head : 128 * (head + 1)].astype(BF)
        for j in range(2):
            for e in range(2):
                at = 256 * e + 64 * j
                out_ref[2 * x + j, 512 + 128 * e : 640 + 128 * e] = jnp.concatenate(
                    [block[:, at : at + 64], block[:, at + 128 : at + 192]], axis=1
                )


def project(me, part, other, g):
    whole = pl.BlockSpec(memory_space=pltpu.VMEM)
    return pl.pallas_call(
        project_kernel,
        in_specs=[pl.BlockSpec(memory_space=pltpu.SMEM), whole, whole, whole],
        out_specs=whole,
        out_shape=jax.ShapeDtypeStruct((8, 768, 128), BF),
        scratch_shapes=[pltpu.VMEM((1536, 512), F32)],
        compiler_params=pltpu.CompilerParams(vmem_limit_bytes=GRANT),
        name="project",
    )(me, part, other, g)


def attend_unit(in_ref, g_ref, mask_ref, out_ref, dk_ref, dv_ref, per, rows, norm_row, outs):
    q0, o0, k0, v0, g0 = rows
    gq0, gk0, gv0 = outs
    group = 256 // per
    keys = 1024
    chunk = 1024
    for b in range(8 // group):
        sources = range(group * b, group * (b + 1))
        q = jnp.concatenate([in_ref[s, q0 : q0 + per] for s in sources], axis=0)
        o = jnp.concatenate([in_ref[s, o0 : o0 + per] for s in sources], axis=0)
        g = g_ref[g0 + 256 * b : g0 + 256 * (b + 1)]
        product = g.astype(F32) * o.astype(F32)
        dots = lax.dot_general(
            jnp.ones((8, 128), F32), product, NT_DIMS, precision=lax.Precision.HIGHEST, preferred_element_type=F32
        )[0:1]
        dots = dots.astype(BF).astype(F32)
        norm = norm_row(b)
        dq = jnp.zeros((HD, 256), F32)
        for n in range(keys // chunk):
            src = slice(chunk // 128 * n, chunk // 128 * (n + 1))
            k = in_ref[src, k0 : k0 + 128].reshape(chunk, HD)
            v = in_ref[src, v0 : v0 + 128].reshape(chunk, HD)
            scores = dot(k, q, NT_DIMS)
            prob = jnp.exp2(scores * (SCALE * LOG2E) - norm)
            allowed = mask_ref[chunk // TILE * n : chunk // TILE * (n + 1), 256 * b : 256 * (b + 1)]
            prob = (prob.reshape(chunk // TILE, TILE, 256) * allowed[:, None, :]).reshape(chunk, 256)
            score_grad = prob * (dot(v, g, NT_DIMS) - dots)
            prob = prob.astype(BF)
            score_grad = score_grad.astype(BF)
            dv = dot(prob, g, NN_DIMS)
            dk = dot(score_grad, q, NN_DIMS)
            at = slice(chunk * n, chunk * (n + 1))
            if b == 0:
                dv_ref[at] = dv
                dk_ref[at] = dk
            else:
                dv_ref[at] += dv
                dk_ref[at] += dk
            dq = dq + dot(k, score_grad, TN_DIMS)
        dq = (dq.T * SCALE).astype(BF)
        for e, s in enumerate(sources):
            out_ref[s, gq0 : gq0 + per] = dq[per * e : per * (e + 1)]
    for s in range(8):
        at = slice(128 * s, 128 * (s + 1))
        out_ref[s, gk0 : gk0 + 128] = (dk_ref[at] * SCALE).astype(BF)
        out_ref[s, gv0 : gv0 + 128] = dv_ref[at].astype(BF)


def attend_kernel(me_ref, *refs):
    sent_refs = refs[:8]
    mid_ref, mask_a_hbm, mask_c_hbm, out_ref, in_ref, g_ref, dk_ref, dv_ref, mask_a_ref, mask_c_ref, sems = refs[8:]
    sources = [ref if d % 2 else ref.at[pl.ds(SLAB, IN_ROWS)] for d, ref in enumerate(sent_refs)]
    targets = [in_ref.at[partner(me_ref, d)] for d in range(8)]
    copies = start((*sources, mask_a_hbm, mask_c_hbm), (*targets, mask_a_ref, mask_c_ref), sems)
    for y in range(2):
        for n in range(6):
            total = mid_ref[y, 128 * n : 128 * (n + 1)].astype(F32)
            for x in range(1, 4):
                total = total + mid_ref[2 * x + y, 128 * n : 128 * (n + 1)].astype(F32)
            total = total.astype(BF).T
            if n < 4:
                at = 128 * (2 * n + y)
                g_ref[at : at + 128] = total
            else:
                for e in range(2):
                    at = 1024 + 64 * (4 * (n - 4) + 2 * e + y)
                    g_ref[at : at + 64] = total[64 * e : 64 * (e + 1)]
    for copy in copies:
        copy.wait()
    second = me_ref[0] % 2 == 1

    def norm_a(b):
        parts = [in_ref[s, NR : NR + 16].astype(F32)[0:1] for s in (2 * b, 2 * b + 1)]
        return jnp.concatenate(parts, axis=1) * LOG2E

    def norm_c(b):
        parts = []
        for s in range(4 * b, 4 * b + 4):
            row = in_ref[s, NR : NR + 16].astype(F32)[1:2]
            parts.append(jnp.where(second, row[:, 64:], row[:, :64]))
        return jnp.concatenate(parts, axis=1) * LOG2E

    attend_unit(
        in_ref, g_ref, mask_a_ref, out_ref, dk_ref, dv_ref, 128, (QA, OA, KA, VA, 0), norm_a, (GQA, GKA, GVA)
    )
    attend_unit(
        in_ref, g_ref, mask_c_ref, out_ref, dk_ref, dv_ref, 64, (QC, OC, KC, VC, 1024), norm_c, (GQC, GKC, GVC)
    )


def attend(me, arrived, partial, mask_a, mask_c):
    whole = pl.BlockSpec(memory_space=pltpu.VMEM)
    return pl.pallas_call(
        attend_kernel,
        in_specs=[pl.BlockSpec(memory_space=pltpu.SMEM)]
        + [pl.BlockSpec(memory_space=pl.ANY)] * 8
        + [whole]
        + [pl.BlockSpec(memory_space=pl.ANY)] * 2,
        out_specs=whole,
        out_shape=jax.ShapeDtypeStruct((8, OUT_ROWS, 128), BF),
        scratch_shapes=[
            pltpu.VMEM((8, IN_ROWS, 128), BF),
            pltpu.VMEM((1536, 128), BF),
            pltpu.VMEM((1024, 128), F32),
            pltpu.VMEM((1024, 128), F32),
            pltpu.VMEM((16, 1024), F32),
            pltpu.VMEM((16, 512), F32),
            pltpu.SemaphoreType.DMA((10,)),
        ],
        compiler_params=pltpu.CompilerParams(vmem_limit_bytes=GRANT),
        name="attend",
    )(me, *arrived, partial, mask_a, mask_c)


def merge_kernel(in_ref, gq_ref, gk_ref, gv_ref):
    for j in range(2):
        own = slice(HD * j, HD * (j + 1))
        gq_ref[0, :, own] = in_ref[j, GQA : GQA + 128]
        gk_ref[0, :, own] = in_ref[j, GKA : GKA + 128]
        gv_ref[0, :, own] = in_ref[j, GVA : GVA + 128]
        gq_ref[0, TILE * j : TILE * (j + 1), 2 * HD :] = in_ref[j, GQC : GQC + 64]
    for ref, at in ((gk_ref, GKC), (gv_ref, GVC)):
        total = in_ref[0, at : at + 128].astype(F32) + in_ref[1, at : at + 128].astype(F32)
        ref[0, :, 2 * HD :] = total.astype(BF)


def merge(arrived):
    out = pl.BlockSpec((1, 128, 3 * HD), lambda i: (0, 0, i))
    shape = jax.ShapeDtypeStruct((1, 128, 1536), BF)
    return pl.pallas_call(
        merge_kernel,
        grid=(4,),
        in_specs=[pl.BlockSpec((2, OUT_ROWS, 128), lambda i: (i, 0, 0))],
        out_specs=(out, out, out),
        out_shape=(shape, shape, shape),
        compiler_params=pltpu.CompilerParams(vmem_limit_bytes=GRANT),
        name="merge",
    )(arrived)


def exchange(array, axes):
    return lax.all_to_all(array, axes, split_axis=0, concat_axis=0, tiled=True)


def spread(array, axes, count):
    return exchange(jnp.broadcast_to(array[None], (count,) + array.shape), axes)


def gather_weight(proj_weight):
    own = spread(proj_weight, "z", 16)
    own = spread(own, ("yh", "yl"), 4).reshape(2, 2, 384, 384)
    other = lax.ppermute(own, "core", [(0, 1), (1, 0)])
    return own, other


def mask_kernel(shared, where_ref, table_ref, out_ref):
    x, y = where_ref[0] // 2, where_ref[0] % 2
    tile = lax.broadcasted_iota(jnp.int32, out_ref.shape, 0)
    group = lax.broadcasted_iota(jnp.int32, out_ref.shape, 1) // TILE
    of_lane = 2 * group + y if shared else group
    head = 3 * x + 2 if shared else 3 * x + y
    out_ref[...] = dot(table_ref[0, head].astype(F32), jnp.where(tile == of_lane, 1.0, 0.0), TN_DIMS)


def mask_rows(me, tile_mask, shared):
    whole = pl.BlockSpec(memory_space=pltpu.VMEM)
    return pl.pallas_call(
        functools.partial(mask_kernel, shared),
        in_specs=[pl.BlockSpec(memory_space=pltpu.SMEM), whole],
        out_specs=whole,
        out_shape=jax.ShapeDtypeStruct((16, 512 if shared else 1024), F32),
        compiler_params=pltpu.CompilerParams(vmem_limit_bytes=GRANT),
        name="mask",
    )(me, tile_mask)


def swap(array, partners):
    pairs = [(8 * core + s, 8 * core + (s ^ partners[core])) for core in range(2) for s in range(8)]
    return lax.ppermute(array, ("core", "x", "yl"), pairs)


def after_weight(q, k, v, o, log_norm, out_grad, own, other, core, tile_mask):
    x, y = lax.axis_index("x"), lax.axis_index("yl")
    me = jnp.stack([2 * x + y, core])
    sent = pack(me, q[0], k[0], v[0], o[0], log_norm[0].T, out_grad[0])
    arrived = [sent[0]] + [swap(sent[d], PARTNERS[d]) for d in range(1, 6)]
    arrived.append(swap(swap(sent[6], (6, 2)), (2, 6)))
    arrived.append(swap(swap(sent[7], (3, 7)), (6, 2)))
    part, slab = project_own(me, own, arrived[::2])
    partial = exchange(project(me, part, other, slab), ("x", "yl"))
    mask_a, mask_c = mask_rows(me, tile_mask, False), mask_rows(me, tile_mask, True)
    result = exchange(attend(me, arrived, partial, mask_a, mask_c), ("x", "yl"))
    return merge(result)


def local(queries, key_states, value_states, attn_out, log_norm, out_grad, proj_weight, tile_mask):
    own, other = gather_weight(proj_weight)
    return after_weight(
        queries,
        key_states,
        value_states,
        attn_out,
        log_norm,
        out_grad,
        own,
        other,
        lax.axis_index("core"),
        tile_mask,
    )


def solution(mesh):
    inner = Mesh(mesh.devices.reshape(16, 2, 2, 4, 2), ("z", "yh", "core", "x", "yl"))
    clips, tokens = ("z", "yh", "core"), ("x", "yl")
    rows = P(clips, tokens, None)
    return jax.shard_map(
        local,
        mesh=inner,
        in_specs=(rows,) * 6 + (P(clips, tokens), P(clips, None, None, None)),
        out_specs=(rows, rows, rows),
        check_vma=False,
    )
```
